256 devices in a mesh: ctx: 64 (over z, y, core), ch: 4 (over x).
Axes of the slice: x: 4, y: 4, z: 8, core: 2. Of those that a mesh axis runs over, the one named last changes fastest.
Arguments:
- conv_input: bfloat16 [256, 128, 8192], P('ctx', None, 'ch'), may hold values from -6 to 6
- gate_signal: bfloat16 [256, 128, 8192], P('ctx', None, 'ch'), may hold values from -6 to 6
- cotangent: bfloat16 [256, 128, 8192], P('ctx', None, 'ch'), may hold values from -6 to 6
- filters: float32 [16, 1024], replicated
- tile_owner: int32 [192], replicated, may hold values from 0 to 63, as said below
- support: int32 [192, 8], replicated, may hold values from -1 to 191, as said below
Outputs:
- gate_grad: bfloat16 [256, 128, 8192], P('ctx', None, 'ch')
- input_grad: bfloat16 [256, 128, 8192], P('ctx', None, 'ch')
- filter_grad: float32 [16, 1024], replicated
The draws below stay inside these ranges and needn't reach their ends.
Inputs may be any that keep to these rules, and one draw needn't show every extreme that they name: tile_owner never falls from one tile to the next; every index of ctx owns from 2 to 4 tiles, some index owns 3 + 1 and some index owns 3 - 1. support[t, k] is t - k where tile t - k belongs to the document of tile t and -1 otherwise; documents are runs of whole tiles, and some document spans 8 tiles or more.
All inputs are finite; a program needn't handle non-finite values.
Results may differ from the reference program's by a relative error of at most 0.0058.
Values may be sent and summed in bfloat16 or wider, within the bound.
No kernel may reach another device: no remote copies, remote signals or barrier semaphores. Data moves between devices by JAX's collectives and lax.ppermute only.
A program may use at most 256 MiB of HBM per device.

```python
import math
import jax
import jax.numpy as jnp
from jax import lax

D = 8192
TILE = 128
GROUP = 128
FILTERS = 16
MAXLAG = 8
TILES_DEV = 3
SLOTS = 4
TILES = 192
STORED = 256
LAGS = 1024
N_CTX = 64


def draw_filters(key, part):
    key_noise = jax.random.fold_in(key, 11)
    key_rate = jax.random.fold_in(key, 12)
    lag_axis = jnp.arange(LAGS, dtype=jnp.float32)
    noise_values = jax.random.normal(key_noise, (FILTERS, LAGS), jnp.float32)
    decay_rate = jnp.exp(jax.random.uniform(key_rate, (FILTERS, 1), jnp.float32, jnp.log(1.0 / (8.0 * LAGS)), jnp.log(1.0 / 40.0)))
    return 0.06 * noise_values * jnp.exp(-lag_axis[None, :] * decay_rate)


def draw_tile_owner(key, part):
    device_total = TILES // TILES_DEV
    pair_count = device_total // 2
    pair_moves = jax.random.randint(jax.random.fold_in(key, 21), (pair_count,), -1, 2)
    pair_moves = pair_moves.at[0].set(1)
    paired = jnp.stack([pair_moves, -pair_moves], axis=1).reshape(device_total)
    shuffle = jax.random.permutation(jax.random.fold_in(key, 22), device_total)
    changes = jnp.zeros((device_total,), jnp.int32).at[shuffle].set(paired.astype(jnp.int32))
    run_ends = jnp.cumsum(TILES_DEV + changes)
    tile_ids = jnp.arange(TILES, dtype=jnp.int32)
    return jnp.sum((tile_ids[:, None] >= run_ends[None, :]).astype(jnp.int32), axis=1).astype(jnp.int32)


def draw_support(key, part):
    tile_ids = jnp.arange(TILES, dtype=jnp.int32)
    starts_doc = jax.random.randint(jax.random.fold_in(key, 31), (TILES,), 0, 4) == 0
    long_end = jax.random.randint(jax.random.fold_in(key, 32), (), MAXLAG - 1, TILES)
    held_open = (tile_ids > long_end - MAXLAG + 1) & (tile_ids <= long_end)
    starts_doc = starts_doc & jnp.logical_not(held_open) | (tile_ids == 0)
    doc_begin = lax.cummax(jnp.where(starts_doc, tile_ids, 0), axis=0)
    lag_ids = jnp.arange(MAXLAG, dtype=jnp.int32)
    source = tile_ids[:, None] - lag_ids[None, :]
    return jnp.where(source >= doc_begin[:, None], source, -1).astype(jnp.int32)


def shard_levels(stream_key, extent, split, smallest, high):
    level, own = 1.0, jax.random.fold_in(stream_key, 6)
    for dim, shards_of in split:
        draws = jnp.exp(jax.random.uniform(jax.random.fold_in(own, dim), (shards_of,), jnp.float32, smallest / len(split), high / len(split)))
        level = level * jnp.repeat(draws, extent[dim] // shards_of).reshape([-1 if axis == dim else 1 for axis in range(len(extent))])
    return level


def bell_draw(rng, extent, spread, bound, cuts=(), kind=jnp.bfloat16):
    drawn = jax.random.normal(rng, extent, jnp.float32) * spread
    if len(cuts) > 0:
        drawn = shard_levels(rng, extent, cuts, -0.22, 0.18) * drawn
    return jnp.clip(drawn, min=-bound, max=bound).astype(kind)


def setup_inputs(seed: int = 0) -> dict:
    arg_keys = jax.random.split(jax.random.key(seed), 7)
    return {
        "conv_input": bell_draw(arg_keys[0], (STORED, TILE, D), 1.0, 6.0, ((0, 64), (2, 4))),
        "gate_signal": bell_draw(arg_keys[1], (STORED, TILE, D), 1.0, 6.0, ((0, 64), (2, 4))),
        "cotangent": bell_draw(arg_keys[2], (STORED, TILE, D), 1.0, 6.0, ((0, 64), (2, 4))),
        "filters": draw_filters(jax.random.fold_in(arg_keys[6], 71), 0),
        "tile_owner": draw_tile_owner(jax.random.fold_in(arg_keys[6], 71), 0),
        "support": draw_support(jax.random.fold_in(arg_keys[6], 71), 0),
    }


def filter_blocks(filters, tile_rows, maxlag):
    narrow = filters.astype(jnp.bfloat16)
    row_ids = jnp.arange(tile_rows, dtype=jnp.int32)
    lag_offsets = jnp.arange(maxlag, dtype=jnp.int32)[:, None, None] * tile_rows + row_ids[:, None] - row_ids[None, :]
    picked = jnp.take(narrow, jnp.clip(lag_offsets, 0, filters.shape[1] - 1), axis=1)
    return jnp.where(lag_offsets[None] >= 0, picked, jnp.zeros_like(picked))

def lag_sums(square):
    filter_count, side_length = (square.shape[0], square.shape[1])
    flipped = square[:, :, ::-1]
    padded = jnp.pad(flipped, ((0, 0), (0, 0), (0, side_length)))
    skewed = padded.reshape(filter_count, 2 * side_length * side_length)[:, :side_length * (2 * side_length - 1)]
    return lax.optimization_barrier(jnp.sum(skewed.reshape(filter_count, side_length, 2 * side_length - 1), axis=1))

def spread_lags(squares, lag_count):
    maxlag, filter_count, side_length = (squares.shape[0], squares.shape[1], squares.shape[2])
    accumulated = jnp.zeros((filter_count, (maxlag + 1) * side_length), jnp.float32)
    for lag_index in range(maxlag):
        start_col = lag_index * side_length
        accumulated = accumulated.at[:, start_col:start_col + 2 * side_length - 1].add(lag_sums(squares[lag_index]))
    return accumulated[:, side_length - 1:side_length - 1 + lag_count]

def reference(conv_input, gate_signal, cotangent, filters, tile_owner, support):
    devices = jnp.arange(N_CTX, dtype=jnp.int32)
    counts = lax.optimization_barrier(jnp.sum((tile_owner[None, :] == devices[:, None]).astype(jnp.int32), axis=1))
    starts = (jnp.cumsum(counts) - counts).astype(jnp.int32)
    tile_ids = jnp.arange(TILES, dtype=jnp.int32)
    stored = (tile_owner * SLOTS + tile_ids - starts[tile_owner]).astype(jnp.int32)
    blocks = filter_blocks(filters, TILE, MAXLAG).astype(jnp.float32)
    valid = support >= 0
    source = jnp.clip(support, 0, TILES - 1).astype(jnp.int32)
    column_span = FILTERS * GROUP

    def one_block(block_index):

        def columns_of(values):
            return lax.dynamic_slice_in_dim(values, block_index * column_span, column_span, 2)[stored]
        signal = columns_of(conv_input).astype(jnp.float32).reshape(TILES, TILE, FILTERS, GROUP)
        cot_part = columns_of(cotangent).astype(jnp.float32)
        gate_part = columns_of(gate_signal).astype(jnp.float32)
        weighted = lax.optimization_barrier((gate_part * cot_part).astype(jnp.bfloat16))
        weighted = weighted.astype(jnp.float32).reshape(TILES, TILE, FILTERS, GROUP)
        conv_out = jnp.zeros((TILES, TILE, FILTERS, GROUP), jnp.float32)
        adjoint = jnp.zeros((TILES, TILE, FILTERS, GROUP), jnp.float32)
        squares = []
        for lag_index in range(MAXLAG):
            valid_rows = valid[:, lag_index][:, None, None, None]
            pieces = jnp.where(valid_rows, signal[source[:, lag_index]], 0.0)
            conv_out = conv_out + jnp.einsum('fij,tjfc->tifc', blocks[:, lag_index], pieces)
            squares.append(jnp.einsum('tifc,tjfc->fij', weighted, pieces))
            adjoint_term = jnp.where(valid_rows, jnp.einsum('fji,tjfc->tifc', blocks[:, lag_index], weighted), 0.0)
            adjoint = adjoint.at[source[:, lag_index]].add(adjoint_term)
        gate_part_grad = (cot_part * conv_out.reshape(TILES, TILE, column_span)).astype(jnp.bfloat16)
        input_part_grad = adjoint.reshape(TILES, TILE, column_span).astype(jnp.bfloat16)
        return (gate_part_grad, input_part_grad, jnp.stack(squares))
    results = lax.map(one_block, jnp.arange(D // column_span, dtype=jnp.int32))
    gate_tiles = jnp.transpose(results[0], (1, 2, 0, 3)).reshape(TILES, TILE, D)
    input_tiles = jnp.transpose(results[1], (1, 2, 0, 3)).reshape(TILES, TILE, D)
    gate_grad = jnp.zeros((N_CTX * SLOTS, TILE, D), jnp.bfloat16).at[stored].set(gate_tiles)
    input_grad = jnp.zeros((N_CTX * SLOTS, TILE, D), jnp.bfloat16).at[stored].set(input_tiles)
    norm_factor = 1.0 / math.sqrt(TILES * TILE * D / FILTERS)
    filter_grad = spread_lags(lax.optimization_barrier(jnp.sum(results[2], axis=0)), LAGS) * norm_factor
    return (gate_grad, input_grad, filter_grad)
```

```python
import functools
import math

import jax
import jax.numpy as jnp
from jax import lax
from jax.experimental import pallas as pl
from jax.experimental.pallas import tpu as pltpu
from jax.sharding import PartitionSpec as P

GROUP = 128
NEAR = 4
BF = jnp.bfloat16
F32 = jnp.float32
VMEM_LIMIT = 60 * 1024 * 1024


def params():
    return pltpu.CompilerParams(vmem_limit_bytes=VMEM_LIMIT)


def shifted(value, axis, steps):
    count = lax.axis_size(axis)
    pairs = [(a, a + steps) for a in range(max(0, -steps), min(count, count - steps))]
    return lax.ppermute(value, axis, pairs)


def swapped(value, axis, mask):
    count = lax.axis_size(axis)
    return lax.ppermute(value, axis, [(a, a ^ mask) for a in range(count)])


def chip_meta(meta):
    first, second, end, core = meta[0], meta[1], meta[2], meta[3]
    return first, second - first, end - first, core


def place(meta, index):
    _, low, _, core = chip_meta(meta)
    on_second = (index >= low).astype(jnp.int32)
    slot = jnp.clip(index - on_second * low, 0, 3)
    return on_second == core, slot


def prep_body(meta, gate, cot, x, w_out, send_out, cot_out):
    half = cot.shape[2] // 2
    w = (gate[0].astype(F32) * cot[0].astype(F32)).astype(BF)
    w_out[0] = w
    other = pl.ds(pl.multiple_of((1 - meta[3]) * half, half), half)
    send_out[0, 0] = x[0, :, other]
    send_out[1, 0] = w_out[0, :, other]
    cot_out[0] = cot[0, :, other]


def prep(meta, gate, cot, x):
    slots, rows, width = x.shape
    half = width // 2
    full = pl.BlockSpec((1, rows, width), lambda s, m: (s, 0, 0))
    return pl.pallas_call(
        prep_body,
        grid_spec=pltpu.PrefetchScalarGridSpec(
            num_scalar_prefetch=1,
            grid=(slots,),
            in_specs=[full, full, full],
            out_specs=[
                full,
                pl.BlockSpec((2, 1, rows, half), lambda s, m: (0, s, 0, 0)),
                pl.BlockSpec((1, rows, half), lambda s, m: (s, 0, 0)),
            ],
        ),
        out_shape=[
            jax.ShapeDtypeStruct(x.shape, BF),
            jax.ShapeDtypeStruct((2, slots, rows, half), BF),
            jax.ShapeDtypeStruct((slots, rows, half), BF),
        ],
        compiler_params=params(),
        name="prep",
    )(meta, gate, cot, x)


def pack_body(x_index, w_index, far, meta, xm, xt, wm, wt, *rest):
    if far:
        xh, wh, x_out, w_out = rest
    else:
        x_out, w_out = rest
    step = pl.program_id(0)
    _, _, count, _ = chip_meta(meta)
    xi = x_index(step, count)
    mine, _ = place(meta, xi)
    value = jnp.where(mine, xm[0], xt[0, 0])
    if far:
        value = jnp.where(xi < 0, xh[0], value)
    x_out[0] = value
    wi = w_index(step, count)
    mine, _ = place(meta, wi)
    value = jnp.where(mine, wm[0], wt[0, 0])
    if far:
        value = jnp.where(wi >= count, wh[0], value)
    w_out[0] = value


def pack(meta, x, w, theirs, tiles, x_index, w_index, x_halo=None, w_halo=None):
    slots, rows, width = x.shape
    half = width // 2
    far = x_halo is not None

    def own(index):
        def at(s, m):
            return (place(m, index(s, m[2] - m[0]))[1], 0, m[3])

        return pl.BlockSpec((1, rows, half), at)

    def other(which, index):
        def at(s, m):
            return (which, place(m, index(s, m[2] - m[0]))[1], 0, 0)

        return pl.BlockSpec((1, 1, rows, half), at)

    specs = [own(x_index), other(0, x_index), own(w_index), other(1, w_index)]
    args = [x, theirs, w, theirs]
    if far:
        specs += [
            pl.BlockSpec((1, rows, half), lambda s, m: (jnp.clip(x_index(s, m[2] - m[0]) + NEAR, 0, NEAR - 1), 0, 0)),
            pl.BlockSpec((1, rows, half), lambda s, m: (jnp.clip(w_index(s, m[2] - m[0]) - (m[2] - m[0]), 0, NEAR - 1), 0, 0)),
        ]
        args += [x_halo, w_halo]
    out = pl.BlockSpec((1, rows, half), lambda s, m: (s, 0, 0))
    return pl.pallas_call(
        functools.partial(pack_body, x_index, w_index, far),
        grid_spec=pltpu.PrefetchScalarGridSpec(
            num_scalar_prefetch=1, grid=(tiles,), in_specs=specs, out_specs=[out, out]
        ),
        out_shape=[jax.ShapeDtypeStruct((tiles, rows, half), BF)] * 2,
        compiler_params=params(),
        name="pack",
    )(meta, *args)


def readers_of(sup, tile, total, lags):
    found = jnp.int32(0)
    for lag in range(lags):
        at = jnp.clip(tile + lag, 0, total - 1)
        live = (tile >= 0) & (tile + lag < total) & (sup[at, lag] >= 0)
        found += live.astype(jnp.int32)
    return found


def sources_of(sup, tile, total, lags):
    at = jnp.clip(tile, 0, total - 1)
    found = jnp.int32(0)
    for lag in range(lags):
        found += (sup[at, lag] >= 0).astype(jnp.int32)
    return found


def column_mask(width, low, high):
    lane = lax.broadcasted_iota(jnp.int32, (16, width), 1)
    return jnp.where((lane >= low) & (lane < high), 1.0, 0.0).astype(BF)


def masked(value, mask):
    rows, width = value.shape
    return (value.reshape(rows // 16, 16, width) * mask[None]).reshape(rows, width)


def dot(a, b):
    return jnp.dot(a, b, preferred_element_type=F32)


def dot_nt(a, b):
    return lax.dot_general(a, b, (((1,), (1,)), ((), ())), preferred_element_type=F32)


def reversal(rows):
    r = lax.broadcasted_iota(jnp.int32, (rows, rows), 0)
    c = lax.broadcasted_iota(jnp.int32, (rows, rows), 1)
    return jnp.where(r + c == rows - 1, 1.0, 0.0).astype(BF)


def diagonal_sums(square):
    rows, width = square.shape
    padded = jnp.concatenate([square, jnp.zeros((rows, rows), F32)], axis=1)
    skewed = pltpu.roll(padded, 0, 1, stride=1, stride_axis=0)
    total = jnp.sum(skewed, axis=0, keepdims=True)
    total = pltpu.roll(jnp.broadcast_to(total, (8, width + rows)), width + 1, 1)
    return total[:1, :width]


def pick(mine, theirs, meta, index):
    own, slot = place(meta, index)
    return jnp.where(own, mine[slot], theirs[slot])


def own_body(lags, total, meta, sup, filt, flip, x, xt, w, wt,
             conv_out, adj_out, sums_out, fwd_out, bwd_out, xs, xl, ws, wl, masks, reach):
    group = pl.program_id(0)
    rows = xs.shape[1]
    cap = xs.shape[0]
    first, _, count, _ = chip_meta(meta)

    @pl.when(group == 0)
    def _():
        for s in range(cap):
            reach[s] = jnp.minimum(readers_of(sup, first + s, total, lags), count - s)
            reach[cap + s] = sources_of(sup, first + s, total, lags)
        for k in range(lags):
            for s in range(cap):
                live = jnp.where(k < reach[s], 1.0, 0.0)
                masks[k, :, s * rows : (s + 1) * rows] = jnp.full((16, rows), live, F32).astype(BF)

    taps = filt[pl.ds(group, 1), :].astype(BF).astype(F32)
    width = taps.shape[1]
    pad = jnp.zeros((1, rows), F32)
    spread = jnp.broadcast_to(jnp.concatenate([taps, pad], axis=1), (rows, width + rows))
    bwd_out[0] = pltpu.roll(spread, 0, 1, stride=1, stride_axis=0)[:, :width].astype(BF)
    taps = flip[pl.ds(group, 1), :].astype(BF).astype(F32)
    spread = jnp.broadcast_to(jnp.concatenate([taps, pad], axis=1), (rows, width + rows))
    fwd_out[0] = pltpu.roll(spread, width + 1, 1, stride=1, stride_axis=0)[:, :width].astype(BF)

    for s in range(cap):
        tile = pick(x, xt.at[0], meta, s)
        xs[s] = tile
        xl[:, s * rows : (s + 1) * rows] = tile
        tile = pick(w, wt.at[0], meta, s)
        ws[s] = tile
        wl[:, s * rows : (s + 1) * rows] = tile
    for i in range(cap):
        near = column_mask(width, (lags - reach[cap + i]) * rows, width)[:, (lags - 1 - i) * rows :]
        left = masked(fwd_out[0, :, (lags - 1 - i) * rows :], near)
        conv_out[i] = dot(left, xs[0 : i + 1].reshape((i + 1) * rows, rows))
    for s in range(cap):
        size = (cap - s) * rows
        left = masked(bwd_out[0, :, :size], column_mask(size, 0, reach[s] * rows))
        adj_out[s] = dot(left, ws[s:cap].reshape(size, rows))
    turned = dot(reversal(rows), xl[...]).astype(BF)
    squares = []
    for k in range(lags):
        size = (cap - k) * rows
        left = masked(turned[:, :size], masks[k, :, :size])
        squares.append(dot_nt(left, wl[:, k * rows :]))
    sums_out[pl.ds(group, 1), :] = diagonal_sums(jnp.concatenate(squares, axis=1))


def own_pairs(meta, sup, filt, flip, x, w, theirs, lags):
    slots, rows, width = x.shape
    half = width // 2
    groups = half // GROUP
    total = sup.shape[0]
    taps = filt.shape[1]
    cap = 2 * slots

    def lane(g, m, s):
        return (0, 0, m[3] * groups + g)

    in_specs = [
        pl.BlockSpec((groups, taps), lambda g, m, s: (m[3], 0)),
        pl.BlockSpec((groups, taps), lambda g, m, s: (m[3], 0)),
        pl.BlockSpec((slots, rows, GROUP), lane),
        pl.BlockSpec((1, slots, rows, GROUP), lambda g, m, s: (0, 0, 0, g)),
        pl.BlockSpec((slots, rows, GROUP), lane),
        pl.BlockSpec((1, slots, rows, GROUP), lambda g, m, s: (1, 0, 0, g)),
    ]
    tiles = pl.BlockSpec((cap, rows, GROUP), lambda g, m, s: (0, 0, g))
    bands = pl.BlockSpec((1, rows, taps), lambda g, m, s: (g, 0, 0))
    return pl.pallas_call(
        functools.partial(own_body, lags, total),
        grid_spec=pltpu.PrefetchScalarGridSpec(
            num_scalar_prefetch=2,
            grid=(groups,),
            in_specs=in_specs,
            out_specs=[tiles, tiles, pl.BlockSpec((groups, taps), lambda g, m, s: (0, 0)), bands, bands],
            scratch_shapes=[
                pltpu.VMEM((cap, rows, GROUP), BF),
                pltpu.VMEM((rows, cap * GROUP), BF),
                pltpu.VMEM((cap, rows, GROUP), BF),
                pltpu.VMEM((rows, cap * GROUP), BF),
                pltpu.VMEM((lags, 16, cap * GROUP), BF),
                pltpu.SMEM((2 * cap,), jnp.int32),
            ],
        ),
        out_shape=[
            jax.ShapeDtypeStruct((cap, rows, half), F32),
            jax.ShapeDtypeStruct((cap, rows, half), F32),
            jax.ShapeDtypeStruct((groups, taps), F32),
            jax.ShapeDtypeStruct((groups, rows, taps), BF),
            jax.ShapeDtypeStruct((groups, rows, taps), BF),
        ],
        compiler_params=params(),
        cost_estimate=pl.CostEstimate(flops=8_000_000_000, bytes_accessed=16 << 20, transcendentals=0),
        name="own_pairs",
    )(meta, sup, filt, flip, x, theirs, w, theirs)


def cross_body(lags, total, meta, sup, prior, x, xt, w, wt, xh, wh, sums_out, xl, wl, masks):
    group = pl.program_id(0)
    rows = xl.shape[0]
    spots = xl.shape[1] // rows
    cap = spots - NEAR
    first, _, count, _ = chip_meta(meta)

    @pl.when(group == 0)
    def _():
        for p in range(spots):
            s = p - NEAR
            found = readers_of(sup, first + s, total, lags)
            deep = s <= count - NEAR - 1
            for k in range(lags):
                t = s + k
                if s < 0:
                    live = (t >= 0) & (deep | (t < count))
                else:
                    live = deep & (t >= count)
                live = live & (k < found)
                masks[k, :, p * rows : (p + 1) * rows] = jnp.full((16, rows), jnp.where(live, 1.0, 0.0), F32).astype(BF)

    for p in range(NEAR):
        xl[:, p * rows : (p + 1) * rows] = xh[p]
    for s in range(cap):
        xl[:, (s + NEAR) * rows : (s + NEAR + 1) * rows] = pick(x, xt.at[0], meta, s)
    for t in range(spots):
        own = pick(w, wt.at[0], meta, t)
        wl[:, t * rows : (t + 1) * rows] = jnp.where(t < count, own, wh[jnp.clip(t - count, 0, NEAR - 1)])
    turned = dot(reversal(rows), xl[...]).astype(BF)
    squares = []
    for k in range(lags):
        low, high = max(0, NEAR - k), min(spots, spots + NEAR - k)
        left = masked(turned[:, low * rows : high * rows], masks[k, :, low * rows : high * rows])
        squares.append(dot_nt(left, wl[:, (low - NEAR + k) * rows : (high - NEAR + k) * rows]))
    row = pl.ds(group, 1)
    sums_out[row, :] = prior[row, :] + diagonal_sums(jnp.concatenate(squares, axis=1))


def cross_squares(meta, sup, prior, x, w, theirs, x_halo, w_halo, lags):
    slots, rows, width = x.shape
    half = width // 2
    groups = half // GROUP
    taps = prior.shape[1]
    spots = 2 * slots + NEAR

    def lane(g, m, s):
        return (0, 0, m[3] * groups + g)

    halo = pl.BlockSpec((NEAR, rows, GROUP), lambda g, m, s: (0, 0, g))
    whole = pl.BlockSpec((groups, taps), lambda g, m, s: (0, 0))
    return pl.pallas_call(
        functools.partial(cross_body, lags, sup.shape[0]),
        grid_spec=pltpu.PrefetchScalarGridSpec(
            num_scalar_prefetch=2,
            grid=(groups,),
            in_specs=[
                whole,
                pl.BlockSpec((slots, rows, GROUP), lane),
                pl.BlockSpec((1, slots, rows, GROUP), lambda g, m, s: (0, 0, 0, g)),
                pl.BlockSpec((slots, rows, GROUP), lane),
                pl.BlockSpec((1, slots, rows, GROUP), lambda g, m, s: (1, 0, 0, g)),
                halo,
                halo,
            ],
            out_specs=whole,
            scratch_shapes=[
                pltpu.VMEM((rows, spots * GROUP), BF),
                pltpu.VMEM((rows, spots * GROUP), BF),
                pltpu.VMEM((lags, 16, spots * GROUP), BF),
            ],
        ),
        out_shape=jax.ShapeDtypeStruct((groups, taps), F32),
        compiler_params=params(),
        cost_estimate=pl.CostEstimate(flops=3_000_000_000, bytes_accessed=6 << 20, transcendentals=0),
        name="cross_squares",
    )(meta, sup, prior, x, theirs, w, theirs, x_halo, w_halo)


def last_body(lags, total, slots, meta, sup, conv, adj, fwd, bwd, xn, xf, wn, wf, cot, cot_t,
              gate_out, input_out, send_out, xs, ws, reach):
    group = pl.program_id(0)
    rows = conv.shape[1]
    cap = 2 * slots
    first, low, count, core = chip_meta(meta)
    far = lags - 1 - NEAR

    @pl.when(group == 0)
    def _():
        for i in range(lags - 1):
            reach[i] = sources_of(sup, first + i, total, lags)
            reach[lags + i] = readers_of(sup, first + count - 1 - i, total, lags)

    xs[0:far] = xf[...]
    xs[far : lags - 1] = xn[...]
    ws[0:NEAR] = wn[...]
    ws[NEAR : lags - 1] = wf[...]
    for i in range(lags - 1):
        size = (lags - 1 - i) * rows
        mask = column_mask(size, (lags - reach[i]) * rows, lags * rows)
        conv[i] += dot(masked(fwd[0, :, :size], mask), xs[i : lags - 1].reshape(size, rows))
    for c in range(lags - 1):
        s = count - 1 - c
        size = (lags - 1 - c) * rows
        mask = column_mask(size, 0, (reach[lags + c] - 1 - c) * rows)
        term = dot(masked(bwd[0, :, (c + 1) * rows :], mask), ws[0 : lags - 1 - c].reshape(size, rows))

        @pl.when(s >= 0)
        def _():
            adj[jnp.maximum(s, 0)] += term

    high = count - low
    for slot in range(slots):
        for own in (True, False):
            second = core if own else 1 - core
            index = jnp.minimum(slot + second * low, cap - 1)
            live = slot < jnp.where(second == 1, high, low)
            cot_tile = (cot if own else cot_t)[slot]
            grad = jnp.where(live, cot_tile.astype(F32) * conv[index], 0.0).astype(BF)
            back = jnp.where(live, adj[index], 0.0).astype(BF)
            if own:
                gate_out[slot] = grad
                input_out[slot] = back
            else:
                send_out[0, slot] = grad
                send_out[1, slot] = back


def last_pairs(meta, sup, conv, adj, fwd, bwd, xn, xf, wn, wf, cot, cot_theirs, lags):
    slots, rows, width = cot.shape
    half = width // 2
    groups = half // GROUP
    taps = fwd.shape[2]
    far = lags - 1 - NEAR

    def lane(g, m, s):
        return (0, 0, m[3] * groups + g)

    def plain(tiles):
        return pl.BlockSpec((tiles, rows, GROUP), lambda g, m, s: (0, 0, g))

    bands = pl.BlockSpec((1, rows, taps), lambda g, m, s: (g, 0, 0))
    own = pl.BlockSpec((slots, rows, GROUP), lane)
    return pl.pallas_call(
        functools.partial(last_body, lags, sup.shape[0], slots),
        grid_spec=pltpu.PrefetchScalarGridSpec(
            num_scalar_prefetch=2,
            grid=(groups,),
            in_specs=[
                plain(2 * slots),
                plain(2 * slots),
                bands,
                bands,
                plain(NEAR),
                plain(far),
                plain(NEAR),
                plain(far),
                own,
                plain(slots),
            ],
            out_specs=[own, own, pl.BlockSpec((2, slots, rows, GROUP), lambda g, m, s: (0, 0, 0, g))],
            scratch_shapes=[
                pltpu.VMEM((lags - 1, rows, GROUP), BF),
                pltpu.VMEM((lags - 1, rows, GROUP), BF),
                pltpu.SMEM((2 * lags,), jnp.int32),
            ],
        ),
        out_shape=[
            jax.ShapeDtypeStruct(cot.shape, BF),
            jax.ShapeDtypeStruct(cot.shape, BF),
            jax.ShapeDtypeStruct((2, slots, rows, half), BF),
        ],
        compiler_params=params(),
        cost_estimate=pl.CostEstimate(flops=4_000_000_000, bytes_accessed=20 << 20, transcendentals=0),
        name="last_pairs",
    )(meta, sup, conv, adj, fwd, bwd, xn, xf, wn, wf, cot, cot_theirs)


def join(meta, gate, inp, got):
    slots, rows, width = gate.shape
    half = width // 2
    blank = pl.BlockSpec(memory_space=pl.ANY)
    out = pl.BlockSpec((1, rows, half), lambda s, m: (s, 0, 1 - m[3]))
    return pl.pallas_call(
        join_body_blocks,
        grid_spec=pltpu.PrefetchScalarGridSpec(
            num_scalar_prefetch=1,
            grid=(slots,),
            in_specs=[blank, blank, pl.BlockSpec((2, 1, rows, half), lambda s, m: (0, s, 0, 0))],
            out_specs=[out, out],
        ),
        out_shape=[jax.ShapeDtypeStruct(gate.shape, BF)] * 2,
        input_output_aliases={1: 0, 2: 1},
        compiler_params=params(),
        name="join",
    )(meta, gate, inp, got)


def join_body_blocks(meta, gate_in, input_in, got, gate_out, input_out):
    gate_out[0] = got[0, 0]
    input_out[0] = got[1, 0]


def per_device(conv_input, gate_signal, cotangent, filters, tile_owner, support):
    slots, rows, width = conv_input.shape
    lags = support.shape[1]
    filter_count, taps = filters.shape
    total = tile_owner.shape[0]
    me = lax.axis_index("ctx")
    core = me % 2
    entry = jnp.arange(8, dtype=jnp.int32)
    before = jnp.sum((tile_owner[None, :] < (me - core + entry)[:, None]).astype(jnp.int32), axis=1)
    meta = jnp.where(entry == 3, core, before)
    far = lags - 1 - NEAR

    w, send, cot_send = prep(meta, gate_signal, cotangent, conv_input)
    theirs = swapped(send, "ctx", 1)
    xs, ws = pack(meta, conv_input, w, theirs, NEAR, lambda s, n: n - NEAR + s, lambda s, n: s)
    xn = shifted(xs, "ctx", 2)
    wn = shifted(ws, "ctx", -2)
    cot_theirs = swapped(cot_send, "ctx", 1)
    conv, adj, sums, fwd, bwd = own_pairs(
        meta, support, filters, filters[:, ::-1], conv_input, w, theirs, lags
    )
    xn, wn, conv, adj, sums = lax.optimization_barrier((xn, wn, conv, adj, sums))
    xs, ws = pack(
        meta, conv_input, w, theirs, far, lambda s, n: n - NEAR - far + s, lambda s, n: NEAR + s, xn, wn
    )
    xf = shifted(xs, "ctx", 2)
    wf = shifted(ws, "ctx", -2)
    sums = cross_squares(meta, support, sums, conv_input, w, theirs, xn, wn, lags)
    xf, wf, sums = lax.optimization_barrier((xf, wf, sums))
    for mask in (2, 4, 8, 16, 32):
        sums = sums + swapped(sums, "ctx", mask)
    for mask in (1, 2):
        sums = sums + swapped(sums, "ch", mask)
    gate, inp, back = last_pairs(
        meta, support, conv, adj, fwd, bwd, xn, xf, wn, wf, cotangent, cot_theirs, lags
    )
    gate, inp = join(meta, gate, inp, swapped(back, "ctx", 1))
    norm = 1.0 / math.sqrt(total * rows * width * lax.axis_size("ch") / filter_count)
    sums = sums * norm
    partner = swapped(sums, "ctx", 1)
    low = jnp.where(core == 0, sums, partner)
    high = jnp.where(core == 0, partner, sums)
    return gate, inp, jnp.concatenate([low, high], axis=0)


def solution(mesh):
    return jax.shard_map(
        per_device,
        mesh=mesh,
        in_specs=(P("ctx", None, "ch"), P("ctx", None, "ch"), P("ctx", None, "ch"), P(), P(), P()),
        out_specs=(P("ctx", None, "ch"), P("ctx", None, "ch"), P()),
        check_vma=False,
    )
```

```python
import functools
import math

import jax
import jax.numpy as jnp
from jax import lax
from jax.experimental import pallas as pl
from jax.experimental.pallas import tpu as pltpu
from jax.sharding import PartitionSpec as P

GROUP = 128
NEAR = 4
PIECE = 2
BF = jnp.bfloat16
F32 = jnp.float32
VMEM_LIMIT = 20 * 1024 * 1024


def params():
    return pltpu.CompilerParams(vmem_limit_bytes=VMEM_LIMIT)


def shifted(value, axis, steps):
    count = lax.axis_size(axis)
    pairs = [(a, a + steps) for a in range(max(0, -steps), min(count, count - steps))]
    return lax.ppermute(value, axis, pairs)


def swapped(value, axis, mask):
    count = lax.axis_size(axis)
    return lax.ppermute(value, axis, [(a, a ^ mask) for a in range(count)])


def chip_meta(meta):
    first, second, end, core = meta[0], meta[1], meta[2], meta[3]
    return first, second - first, end - first, core


def place(meta, index):
    _, low, _, core = chip_meta(meta)
    on_second = (index >= low).astype(jnp.int32)
    slot = jnp.clip(index - on_second * low, 0, 3)
    return on_second == core, slot


def prep_body(meta, gate, cot, x, cot_all, w_out, send, cot_out, w_other, sems):
    slots, rows, half = w_other.shape
    step = pl.program_id(0)
    other = pl.ds(pl.multiple_of((1 - meta[3]) * half, half), half)
    copies = [
        pltpu.make_async_copy(x.at[:, :, other], send.at[0], sems.at[0]),
        pltpu.make_async_copy(cot_all.at[:, :, other], cot_out, sems.at[1]),
    ]

    @pl.when(step == 0)
    def _():
        for copy in copies:
            copy.start()

    w_out[0] = (gate[0].astype(F32) * cot[0].astype(F32)).astype(BF)
    w_other[step] = w_out[0, :, other]
    pltpu.make_async_copy(w_other.at[step], send.at[1, step], sems.at[2 + step]).start()

    @pl.when(step == slots - 1)
    def _():
        for copy in copies:
            copy.wait()
        for s in range(slots):
            pltpu.make_async_copy(w_other.at[s], send.at[1, s], sems.at[2 + s]).wait()


def prep(meta, gate, cot, x):
    slots, rows, width = x.shape
    half = width // 2
    full = pl.BlockSpec((1, rows, width), lambda s, m: (s, 0, 0))
    loose = pl.BlockSpec(memory_space=pl.ANY)
    return pl.pallas_call(
        prep_body,
        grid_spec=pltpu.PrefetchScalarGridSpec(
            num_scalar_prefetch=1,
            grid=(slots,),
            in_specs=[full, full, loose, loose],
            out_specs=[full, loose, loose],
            scratch_shapes=[
                pltpu.VMEM((slots, rows, half), BF),
                pltpu.SemaphoreType.DMA((2 + slots,)),
            ],
        ),
        out_shape=[
            jax.ShapeDtypeStruct(x.shape, BF),
            jax.ShapeDtypeStruct((2, slots, rows, half), BF),
            jax.ShapeDtypeStruct((slots, rows, half), BF),
        ],
        compiler_params=params(),
        cost_estimate=pl.CostEstimate(flops=2 << 20, bytes_accessed=12 << 20, transcendentals=0),
        name="prep",
    )(meta, gate, cot, x, cot)


def pack_body(tiles, x_at, w_at, halos, meta, x, w, theirs, *rest):
    x_halos, w_halos = rest[:halos], rest[halos : 2 * halos]
    x_out, w_out, sems = rest[2 * halos :]
    half = x_out.shape[2]
    _, _, count, core = chip_meta(meta)
    lanes = pl.ds(pl.multiple_of(core * half, half), half)
    for which, (own, out) in enumerate(((x, x_out), (w, w_out))):
        for j in range(tiles):
            sem = sems.at[which * tiles + j]
            index = (x_at if which == 0 else w_at)(j, count)
            mine, slot = place(meta, index)
            depth = -1 - index if which == 0 else index - count
            here = depth < 0

            @pl.when(here & mine)
            def _():
                pltpu.make_async_copy(own.at[slot, :, lanes], out.at[j], sem).start()

            @pl.when(here & jnp.logical_not(mine))
            def _():
                pltpu.make_async_copy(theirs.at[which, slot], out.at[j], sem).start()

            for h in range(halos):
                halo = (x_halos if which == 0 else w_halos)[h]
                inside = jnp.clip(depth - h * PIECE, 0, PIECE - 1)
                row = PIECE - 1 - inside if which == 0 else inside

                @pl.when((depth >= h * PIECE) & (depth < (h + 1) * PIECE))
                def _():
                    pltpu.make_async_copy(halo.at[row], out.at[j], sem).start()

    for which, out in enumerate((x_out, w_out)):
        for j in range(tiles):
            pltpu.make_async_copy(theirs.at[which, 0], out.at[j], sems.at[which * tiles + j]).wait()


def pack(meta, x, w, theirs, tiles, x_at, w_at, x_halos=(), w_halos=()):
    slots, rows, width = x.shape
    half = width // 2
    halos = len(x_halos)
    loose = pl.BlockSpec(memory_space=pl.ANY)
    return pl.pallas_call(
        functools.partial(pack_body, tiles, x_at, w_at, halos),
        grid_spec=pltpu.PrefetchScalarGridSpec(
            num_scalar_prefetch=1,
            grid=(1,),
            in_specs=[loose] * (3 + 2 * halos),
            out_specs=[loose, loose],
            scratch_shapes=[pltpu.SemaphoreType.DMA((2 * tiles,))],
        ),
        out_shape=[jax.ShapeDtypeStruct((tiles, rows, half), BF)] * 2,
        compiler_params=params(),
        cost_estimate=pl.CostEstimate(flops=0, bytes_accessed=tiles << 20, transcendentals=0),
        name="pack",
    )(meta, x, w, theirs, *x_halos, *w_halos)


def readers_of(sup, tile, total, lags):
    found = jnp.int32(0)
    for lag in range(lags):
        at = jnp.clip(tile + lag, 0, total - 1)
        live = (tile >= 0) & (tile + lag < total) & (sup[at, lag] >= 0)
        found += live.astype(jnp.int32)
    return found


def sources_of(sup, tile, total, lags):
    at = jnp.clip(tile, 0, total - 1)
    found = jnp.int32(0)
    for lag in range(lags):
        found += (sup[at, lag] >= 0).astype(jnp.int32)
    return found


def column_mask(width, low, high):
    lane = lax.broadcasted_iota(jnp.int32, (16, width), 1)
    return jnp.where((lane >= low) & (lane < high), 1.0, 0.0).astype(BF)


def masked(value, mask):
    rows, width = value.shape
    return (value.reshape(rows // 16, 16, width) * mask[None]).reshape(rows, width)


def dot(a, b):
    return jnp.dot(a, b, preferred_element_type=F32)


def reversal(rows):
    r = lax.broadcasted_iota(jnp.int32, (rows, rows), 0)
    c = lax.broadcasted_iota(jnp.int32, (rows, rows), 1)
    return jnp.where(r + c == rows - 1, 1.0, 0.0).astype(BF)


def diagonal_sums(square):
    rows, width = square.shape
    padded = jnp.concatenate([square, jnp.zeros((rows, rows), F32)], axis=1)
    skewed = pltpu.roll(padded, 0, 1, stride=1, stride_axis=0)
    total = jnp.sum(skewed, axis=0, keepdims=True)
    total = pltpu.roll(jnp.broadcast_to(total, (8, width + rows)), width + 1, 1)
    return total[:1, :width]


def pick(mine, theirs, meta, index):
    own, slot = place(meta, index)
    return jnp.where(own, mine[slot], theirs[slot])


def own_body(lags, total, base, chained, meta, sup, filt, flip, x, xt, w, wt, *rest):
    rest = rest[4:] if chained else rest
    conv_out, adj_out, fwd_out, bwd_out, sums_out, xs, xl, ws, turned, masks, reach = rest
    step = pl.program_id(0)
    group = base + step
    cap, rows, _ = xs.shape
    first, _, count, _ = chip_meta(meta)

    @pl.when(step == 0)
    def _():
        sums_out[...] = jnp.zeros_like(sums_out)
        for s in range(cap):
            reach[s] = jnp.minimum(readers_of(sup, first + s, total, lags), count - s)
            reach[cap + s] = sources_of(sup, first + s, total, lags)
        for k in range(lags):
            for s in range(cap):
                live = jnp.where(k < reach[s], 1.0, 0.0)
                masks[k, :, s * rows : (s + 1) * rows] = jnp.full((16, rows), live, F32).astype(BF)

    taps = filt[pl.ds(group, 1), :].astype(BF).astype(F32)
    width = taps.shape[1]
    pad = jnp.zeros((1, rows), F32)
    spread = jnp.broadcast_to(jnp.concatenate([taps, pad], axis=1), (rows, width + rows))
    bwd_out[0] = pltpu.roll(spread, 0, 1, stride=1, stride_axis=0)[:, :width].astype(BF)
    taps = flip[pl.ds(group, 1), :].astype(BF).astype(F32)
    spread = jnp.broadcast_to(jnp.concatenate([taps, pad], axis=1), (rows, width + rows))
    fwd_out[0] = pltpu.roll(spread, width + 1, 1, stride=1, stride_axis=0)[:, :width].astype(BF)

    for s in range(cap):
        tile = pick(x, xt.at[0], meta, s)
        xs[s] = tile
        xl[:, s * rows : (s + 1) * rows] = tile
        tile = pick(w, wt.at[0], meta, s)
        ws[s] = tile
        turned[s] = tile.T
    for i in range(cap):
        near = column_mask((i + 1) * rows, (i + 1 - reach[cap + i]) * rows, width)
        left = masked(fwd_out[0, :, (lags - 1 - i) * rows :], near)
        conv_out[i] = dot(left, xs[0 : i + 1].reshape((i + 1) * rows, rows))
    for s in range(cap):
        size = (cap - s) * rows
        left = masked(bwd_out[0, :, :size], column_mask(size, 0, reach[s] * rows))
        adj_out[s] = dot(left, ws[s:cap].reshape(size, rows))
    back = dot(reversal(rows), xl[...]).astype(BF)
    squares = []
    for k in range(lags):
        size = (cap - k) * rows
        left = masked(back[:, :size], masks[k, :, :size])
        squares.append(dot(left, turned[k:cap].reshape(size, rows)))
    sums_out[pl.ds(group, 1), :] = diagonal_sums(jnp.concatenate(squares, axis=1))


def own_pairs(meta, sup, filt, flip, x, w, theirs, lags, base, steps, prior):
    slots, rows, width = x.shape
    half = width // 2
    groups = half // GROUP
    total = sup.shape[0]
    taps = filt.shape[1]
    cap = 2 * slots

    def lane(g, m, s):
        return (0, 0, m[3] * groups + base + g)

    in_specs = [
        pl.BlockSpec((groups, taps), lambda g, m, s: (m[3], 0)),
        pl.BlockSpec((groups, taps), lambda g, m, s: (m[3], 0)),
        pl.BlockSpec((slots, rows, GROUP), lane),
        pl.BlockSpec((1, slots, rows, GROUP), lambda g, m, s: (0, 0, 0, base + g)),
        pl.BlockSpec((slots, rows, GROUP), lane),
        pl.BlockSpec((1, slots, rows, GROUP), lambda g, m, s: (1, 0, 0, base + g)),
    ]
    args = [filt, flip, x, theirs, w, theirs]
    chained = prior is not None
    aliases = {}
    if chained:
        aliases = {2 + len(args) + i: i for i in range(4)}
        in_specs += [pl.BlockSpec(memory_space=pl.ANY)] * 4
        args += list(prior)
    tiles = pl.BlockSpec((cap, rows, GROUP), lambda g, m, s: (0, 0, base + g))
    bands = pl.BlockSpec((1, rows, taps), lambda g, m, s: (base + g, 0, 0))
    return pl.pallas_call(
        functools.partial(own_body, lags, total, base, chained),
        grid_spec=pltpu.PrefetchScalarGridSpec(
            num_scalar_prefetch=2,
            grid=(steps,),
            in_specs=in_specs,
            out_specs=[tiles, tiles, bands, bands, pl.BlockSpec((groups, taps), lambda g, m, s: (0, 0))],
            scratch_shapes=[
                pltpu.VMEM((cap, rows, GROUP), BF),
                pltpu.VMEM((rows, cap * GROUP), BF),
                pltpu.VMEM((cap, rows, GROUP), BF),
                pltpu.VMEM((cap, GROUP, rows), BF),
                pltpu.VMEM((lags, 16, cap * GROUP), BF),
                pltpu.SMEM((2 * cap,), jnp.int32),
            ],
        ),
        out_shape=[
            jax.ShapeDtypeStruct((cap, rows, half), F32),
            jax.ShapeDtypeStruct((cap, rows, half), F32),
            jax.ShapeDtypeStruct((groups, rows, taps), BF),
            jax.ShapeDtypeStruct((groups, rows, taps), BF),
            jax.ShapeDtypeStruct((groups, taps), F32),
        ],
        input_output_aliases=aliases,
        compiler_params=params(),
        cost_estimate=pl.CostEstimate(flops=steps * 1_000_000_000, bytes_accessed=steps << 21, transcendentals=0),
        name="own_pairs",
    )(meta, sup, *args)


def cross_body(lags, total, meta, sup, prior, more, x, xt, w, wt, xn, xm, wn, wm, sums_out, xl, near, deep, masks):
    group = pl.program_id(0)
    rows = xl.shape[0]
    blocks = lags - 1
    first, _, count, _ = chip_meta(meta)
    split = blocks - NEAR

    @pl.when(group == 0)
    def _():
        for p in range(blocks):
            s = p - blocks if p >= split else count - 1 - (blocks - 1 - p)
            found = readers_of(sup, first + s, total, lags)
            if p < split:
                found = jnp.where(s >= 0, found, 0)
            for k in range(lags):
                live = jnp.where(k < found, 1.0, 0.0)
                masks[k, :, p * rows : (p + 1) * rows] = jnp.full((16, rows), live, F32).astype(BF)

    for p in range(split):
        xl[:, p * rows : (p + 1) * rows] = pick(x, xt.at[0], meta, count - 1 - (blocks - 1 - p))
    for p in range(PIECE):
        xl[:, (split + p) * rows : (split + p + 1) * rows] = xm[p]
        xl[:, (split + PIECE + p) * rows : (split + PIECE + p + 1) * rows] = xn[p]
    for t in range(blocks):
        own = pick(w, wt.at[0], meta, t)
        above = jnp.clip(t - count, 0, NEAR - 1)
        halo = jnp.where(above < PIECE, wn[jnp.minimum(above, PIECE - 1)], wm[jnp.maximum(above - PIECE, 0)])
        near[t] = jnp.where(t < count, own, halo).T
    for a in range(split):
        deep[a] = (wn[a] if a < PIECE else wm[a - PIECE]).T
    back = dot(reversal(rows), xl[...]).astype(BF)
    squares = [jnp.zeros((rows, rows), F32)]
    for k in range(1, lags):
        size = min(NEAR, k)
        low = (blocks - size) * rows
        left = masked(back[:, low:], masks[k, :, low:])
        square = dot(left, near[k - size : k].reshape(size * rows, rows))
        size = k - NEAR
        if size > 0:
            low = (split - size) * rows
            left = masked(back[:, low : split * rows], masks[k, :, low : split * rows])
            square += dot(left, deep[0:size].reshape(size * rows, rows))
        squares.append(square)
    row = pl.ds(group, 1)
    sums_out[row, :] = prior[row, :] + more[row, :] + diagonal_sums(jnp.concatenate(squares, axis=1))


def cross_squares(meta, sup, prior, more, x, w, theirs, x_halos, w_halos, lags):
    slots, rows, width = x.shape
    half = width // 2
    groups = half // GROUP
    taps = prior.shape[1]
    blocks = lags - 1

    def lane(g, m, s):
        return (0, 0, m[3] * groups + g)

    halo = pl.BlockSpec((PIECE, rows, GROUP), lambda g, m, s: (0, 0, g))
    whole = pl.BlockSpec((groups, taps), lambda g, m, s: (0, 0))
    return pl.pallas_call(
        functools.partial(cross_body, lags, sup.shape[0]),
        grid_spec=pltpu.PrefetchScalarGridSpec(
            num_scalar_prefetch=2,
            grid=(groups,),
            in_specs=[
                whole,
                whole,
                pl.BlockSpec((slots, rows, GROUP), lane),
                pl.BlockSpec((1, slots, rows, GROUP), lambda g, m, s: (0, 0, 0, g)),
                pl.BlockSpec((slots, rows, GROUP), lane),
                pl.BlockSpec((1, slots, rows, GROUP), lambda g, m, s: (1, 0, 0, g)),
                halo,
                halo,
                halo,
                halo,
            ],
            out_specs=whole,
            scratch_shapes=[
                pltpu.VMEM((rows, blocks * GROUP), BF),
                pltpu.VMEM((blocks, GROUP, rows), BF),
                pltpu.VMEM((blocks - NEAR, GROUP, rows), BF),
                pltpu.VMEM((lags, 16, blocks * GROUP), BF),
            ],
        ),
        out_shape=jax.ShapeDtypeStruct((groups, taps), F32),
        compiler_params=params(),
        cost_estimate=pl.CostEstimate(flops=3_000_000_000, bytes_accessed=6 << 20, transcendentals=0),
        name="cross_squares",
    )(meta, sup, prior, more, x, theirs, w, theirs, *x_halos, *w_halos)


def near_body(lags, total, slots, chained, meta, sup, conv, adj, fwd, bwd, xn, xm, wn, wm, cot, cot_t, *rest):
    rest = rest[5:] if chained else rest
    gate_out, input_out, send_out, conv_out, adj_out, xs, ws, reach = rest
    step = pl.program_id(0)
    rows = conv.shape[1]
    cap = 2 * slots
    first, low, count, core = chip_meta(meta)
    blocks = lags - 1

    @pl.when(step == 0)
    def _():
        for i in range(blocks):
            reach[i] = sources_of(sup, first + i, total, lags)
            reach[lags + i] = readers_of(sup, first + count - 1 - i, total, lags)

    xs[0:PIECE] = xm[...]
    xs[PIECE:NEAR] = xn[...]
    ws[0:PIECE] = wn[...]
    ws[PIECE:NEAR] = wm[...]
    for i in range(blocks):
        farthest = min(blocks, i + NEAR)
        start = (blocks - farthest) * rows
        size = (farthest - i) * rows
        mask = column_mask(size, (lags - reach[i]) * rows - start, lags * rows)
        left = masked(fwd[0, :, start : start + size], mask)
        conv[i] += dot(left, xs[i + NEAR - farthest : NEAR].reshape(size, rows))
    for c in range(blocks):
        s = count - 1 - c
        tiles = min(NEAR, blocks - c)
        size = tiles * rows
        start = (c + 1) * rows
        mask = column_mask(size, 0, reach[lags + c] * rows - start)
        term = dot(masked(bwd[0, :, start : start + size], mask), ws[0:tiles].reshape(size, rows))

        @pl.when(s >= 0)
        def _():
            adj[jnp.maximum(s, 0)] += term

    for i in range(blocks - NEAR):
        conv_out[i] = conv[i]
        adj_out[i] = adj[jnp.maximum(count - 1 - i, 0)]
    high = count - low
    for slot in range(slots):
        for own in (True, False):
            second = core if own else 1 - core
            index = jnp.minimum(slot + second * low, cap - 1)
            live = slot < jnp.where(second == 1, high, low)
            cot_tile = (cot if own else cot_t)[slot]
            grad = jnp.where(live, cot_tile.astype(F32) * conv[index], 0.0).astype(BF)
            back = jnp.where(live, adj[index], 0.0).astype(BF)
            if own:
                gate_out[slot] = grad
                input_out[slot] = back
            else:
                send_out[0, slot] = grad
                send_out[1, slot] = back


def near_pairs(meta, sup, conv, adj, fwd, bwd, x_halos, w_halos, cot, cot_theirs, lags, base, steps, prior):
    slots, rows, width = cot.shape
    half = width // 2
    groups = half // GROUP
    taps = fwd.shape[2]
    far = lags - 1 - NEAR

    def lane(g, m, s):
        return (0, 0, m[3] * groups + base + g)

    def plain(tiles):
        return pl.BlockSpec((tiles, rows, GROUP), lambda g, m, s: (0, 0, base + g))

    bands = pl.BlockSpec((1, rows, taps), lambda g, m, s: (base + g, 0, 0))
    own = pl.BlockSpec((slots, rows, GROUP), lane)
    in_specs = [plain(2 * slots), plain(2 * slots), bands, bands] + [plain(PIECE)] * 4 + [own, plain(slots)]
    args = [conv, adj, fwd, bwd, *x_halos, *w_halos, cot, cot_theirs]
    chained = prior is not None
    aliases = {}
    if chained:
        aliases = {2 + len(args) + i: i for i in range(5)}
        in_specs += [pl.BlockSpec(memory_space=pl.ANY)] * 5
        args += list(prior)
    return pl.pallas_call(
        functools.partial(near_body, lags, sup.shape[0], slots, chained),
        grid_spec=pltpu.PrefetchScalarGridSpec(
            num_scalar_prefetch=2,
            grid=(steps,),
            in_specs=in_specs,
            out_specs=[
                own,
                own,
                pl.BlockSpec((2, slots, rows, GROUP), lambda g, m, s: (0, 0, 0, base + g)),
                plain(far),
                plain(far),
            ],
            scratch_shapes=[
                pltpu.VMEM((NEAR, rows, GROUP), BF),
                pltpu.VMEM((NEAR, rows, GROUP), BF),
                pltpu.SMEM((2 * lags,), jnp.int32),
            ],
        ),
        out_shape=[
            jax.ShapeDtypeStruct(cot.shape, BF),
            jax.ShapeDtypeStruct(cot.shape, BF),
            jax.ShapeDtypeStruct((2, slots, rows, half), BF),
            jax.ShapeDtypeStruct((far, rows, half), F32),
            jax.ShapeDtypeStruct((far, rows, half), F32),
        ],
        input_output_aliases=aliases,
        compiler_params=params(),
        cost_estimate=pl.CostEstimate(flops=steps * 400_000_000, bytes_accessed=steps << 21, transcendentals=0),
        name="near_pairs",
    )(meta, sup, *args)


def far_body(lags, total, meta, sup, conv, adj, fwd, bwd, xa, xb, wa, wb, cot, cot_t, gate_in, input_in, send_in,
             gate_out, input_out, send_out, xs, ws, done, reach, sems):
    step = pl.program_id(0)
    far, rows, half = done.shape[0] // 2, done.shape[1], done.shape[2]
    first, _, count, core = chip_meta(meta)

    @pl.when(step == 0)
    def _():
        for i in range(far):
            reach[i] = sources_of(sup, first + i, total, lags)
            reach[lags + i] = readers_of(sup, first + count - 1 - i, total, lags)

    xs[0 : far - PIECE] = xb[...]
    xs[far - PIECE : far] = xa[...]
    ws[0:PIECE] = wa[...]
    ws[PIECE:far] = wb[...]
    lanes = pl.ds(pl.multiple_of(step * GROUP, GROUP), GROUP)
    for i in range(far):
        size = (far - i) * rows
        mask = column_mask(size, (lags - reach[i]) * rows, lags * rows)
        total_conv = conv[i] + dot(masked(fwd[0, :, :size], mask), xs[i:far].reshape(size, rows))
        done[i, :, lanes] = (pick(cot, cot_t, meta, i).astype(F32) * total_conv).astype(BF)
    for c in range(far):
        start = (c + NEAR + 1) * rows
        size = (far - c) * rows
        mask = column_mask(size, 0, reach[lags + c] * rows - start)
        term = dot(masked(bwd[0, :, start:], mask), ws[0 : far - c].reshape(size, rows))
        done[far + c, :, lanes] = (adj[c] + term).astype(BF)

    @pl.when(step == pl.num_programs(0) - 1)
    def _():
        home = pl.ds(pl.multiple_of(core * half, half), half)
        for r in range(2 * far):
            index = r if r < far else count - 1 - (r - far)
            mine, slot = place(meta, index)
            out = gate_out if r < far else input_out

            @pl.when(mine)
            def _():
                pltpu.make_async_copy(done.at[r], out.at[slot, :, home], sems.at[r]).start()

            @pl.when(jnp.logical_not(mine))
            def _():
                pltpu.make_async_copy(done.at[r], send_out.at[r // far, slot], sems.at[r]).start()

        for r in range(2 * far):
            pltpu.make_async_copy(done.at[r], send_out.at[r // far, 0], sems.at[r]).wait()


def far_pairs(meta, sup, conv, adj, fwd, bwd, x_halos, w_halos, cot, cot_theirs, gate, inp, send, lags):
    slots, rows, width = cot.shape
    half = width // 2
    groups = half // GROUP
    taps = fwd.shape[2]
    far = lags - 1 - NEAR

    def plain(tiles):
        return pl.BlockSpec((tiles, rows, GROUP), lambda g, m, s: (0, 0, g))

    bands = pl.BlockSpec((1, rows, taps), lambda g, m, s: (g, 0, 0))
    own = pl.BlockSpec((slots, rows, GROUP), lambda g, m, s: (0, 0, m[3] * groups + g))
    loose = pl.BlockSpec(memory_space=pl.ANY)
    return pl.pallas_call(
        functools.partial(far_body, lags, sup.shape[0]),
        grid_spec=pltpu.PrefetchScalarGridSpec(
            num_scalar_prefetch=2,
            grid=(groups,),
            in_specs=[
                plain(far),
                plain(far),
                bands,
                bands,
                plain(PIECE),
                plain(far - PIECE),
                plain(PIECE),
                plain(far - PIECE),
                own,
                plain(slots),
                loose,
                loose,
                loose,
            ],
            out_specs=[loose, loose, loose],
            scratch_shapes=[
                pltpu.VMEM((far, rows, GROUP), BF),
                pltpu.VMEM((far, rows, GROUP), BF),
                pltpu.VMEM((2 * far, rows, half), BF),
                pltpu.SMEM((2 * lags,), jnp.int32),
                pltpu.SemaphoreType.DMA((2 * far,)),
            ],
        ),
        out_shape=[
            jax.ShapeDtypeStruct(gate.shape, BF),
            jax.ShapeDtypeStruct(inp.shape, BF),
            jax.ShapeDtypeStruct(send.shape, BF),
        ],
        input_output_aliases={12: 0, 13: 1, 14: 2},
        compiler_params=params(),
        cost_estimate=pl.CostEstimate(flops=800_000_000, bytes_accessed=8 << 20, transcendentals=0),
        name="far_pairs",
    )(meta, sup, conv, adj, fwd, bwd, *x_halos, *w_halos, cot, cot_theirs, gate, inp, send)


def join_body(meta, gate_in, input_in, got, gate_out, input_out, sems):
    half = got.shape[3]
    other = pl.ds(pl.multiple_of((1 - meta[3]) * half, half), half)
    copies = [
        pltpu.make_async_copy(got.at[0], gate_out.at[:, :, other], sems.at[0]),
        pltpu.make_async_copy(got.at[1], input_out.at[:, :, other], sems.at[1]),
    ]
    for copy in copies:
        copy.start()
    for copy in copies:
        copy.wait()


def join(meta, gate, inp, got):
    loose = pl.BlockSpec(memory_space=pl.ANY)
    return pl.pallas_call(
        join_body,
        grid_spec=pltpu.PrefetchScalarGridSpec(
            num_scalar_prefetch=1,
            grid=(1,),
            in_specs=[loose, loose, loose],
            out_specs=[loose, loose],
            scratch_shapes=[pltpu.SemaphoreType.DMA((2,))],
        ),
        out_shape=[jax.ShapeDtypeStruct(gate.shape, BF)] * 2,
        input_output_aliases={1: 0, 2: 1},
        compiler_params=params(),
        name="join",
    )(meta, gate, inp, got)


def per_device(conv_input, gate_signal, cotangent, filters, tile_owner, support):
    slots, rows, width = conv_input.shape
    lags = support.shape[1]
    filter_count, taps = filters.shape
    total = tile_owner.shape[0]
    tie = lax.optimization_barrier
    me = lax.axis_index("ctx")
    core = me % 2
    entry = jnp.arange(8, dtype=jnp.int32)
    before = jnp.sum((tile_owner[None, :] < (me - core + entry)[:, None]).astype(jnp.int32), axis=1)
    meta = jnp.where(entry == 3, core, before)

    def up(value):
        return shifted(value, "ctx", 2)

    def down(value):
        return shifted(value, "ctx", -2)

    w, send, cot_send = prep(meta, gate_signal, cotangent, conv_input)
    theirs = swapped(send, "ctx", 1)
    x, flip = conv_input, filters[:, ::-1]
    xs, ws = pack(meta, x, w, theirs, 2, lambda j, n: n - 2 + j, lambda j, n: j)
    x0, w0 = up(xs), down(ws)
    xs, ws = pack(meta, x, w, theirs, 2, lambda j, n: n - 4 + j, lambda j, n: 2 + j)
    x1, w1 = up(xs), down(ws)
    cot_theirs = swapped(cot_send, "ctx", 1)
    half_groups = width // 2 // GROUP // 2
    one = own_pairs(meta, support, filters, flip, x, w, theirs, lags, 0, half_groups, None)
    x0, w0, one = tie((x0, w0, one))
    xs, ws = pack(meta, x, w, theirs, 2, lambda j, n: n - 6 + j, lambda j, n: 4 + j, (x0,), (w0,))
    xs, ws, one = tie((xs, ws, one))
    x2, w2 = up(xs), down(ws)
    *parts, first_sums = one
    *parts, sums = own_pairs(
        meta, support, filters, flip, x, w, theirs, lags, half_groups, half_groups, parts
    )
    x1, w1, parts, sums = tie((x1, w1, parts, sums))
    conv, adj, fwd, bwd = parts
    sums = cross_squares(meta, support, sums, first_sums, x, w, theirs, (x0, x1), (w0, w1), lags)

    def step(sums, axis, mask, filler):
        moved = swapped(sums, axis, mask)
        if filler is None:
            return sums + moved, None
        sums, out = tie((sums + moved, filler(sums)))
        return sums, out

    def relay(sums):
        _, a, b = tie((sums, x0, x1))
        return pack(meta, x, w, theirs, 1, lambda j, n: n - 7 + j, lambda j, n: 6 + j, (a, b), (w0, w1))

    sums, (xs, ws) = step(sums, "ctx", 2, relay)
    x3, w3 = up(xs), down(ws)

    def close(base, prior):
        def run(sums):
            _, c = tie((sums, conv))
            return near_pairs(
                meta, support, c, adj, fwd, bwd, (x0, x1), (w0, w1), cotangent, cot_theirs, lags,
                base, half_groups, prior,
            )

        return run

    sums, near = step(sums, "ctx", 4, close(0, None))
    sums, near = step(sums, "ch", 1, close(half_groups, near))
    gate, inp, back, conv, adj = near
    sums, _ = step(sums, "ch", 2, None)

    def finish(sums):
        _, c = tie((sums, conv))
        return far_pairs(
            meta, support, c, adj, fwd, bwd, (x2, x3), (w2, w3), cotangent, cot_theirs, gate, inp, back, lags
        )

    sums, (gate, inp, back) = step(sums, "ctx", 8, finish)
    got = swapped(back, "ctx", 1)
    sums, _ = step(sums, "ctx", 16, None)
    sums, _ = step(sums, "ctx", 32, None)
    gate, inp = join(meta, gate, inp, got)
    norm = 1.0 / math.sqrt(total * rows * width * lax.axis_size("ch") / filter_count)
    sums = sums * norm
    partner = swapped(sums, "ctx", 1)
    low = jnp.where(core == 0, sums, partner)
    high = jnp.where(core == 0, partner, sums)
    return gate, inp, jnp.concatenate([low, high], axis=0)


def solution(mesh):
    return jax.shard_map(
        per_device,
        mesh=mesh,
        in_specs=(P("ctx", None, "ch"), P("ctx", None, "ch"), P("ctx", None, "ch"), P(), P(), P()),
        out_specs=(P("ctx", None, "ch"), P("ctx", None, "ch"), P()),
        check_vma=False,
    )
```

```python
import functools
import math

import jax
import jax.numpy as jnp
from jax import lax
from jax.experimental import pallas as pl
from jax.experimental.pallas import tpu as pltpu
from jax.sharding import PartitionSpec as P

GROUP = 128
NEAR = 4
PIECE = 4
BF = jnp.bfloat16
F32 = jnp.float32
VMEM_LIMIT = 8 * 1024 * 1024


def params():
    return pltpu.CompilerParams(vmem_limit_bytes=VMEM_LIMIT)


def shifted(value, axis, steps):
    count = lax.axis_size(axis)
    pairs = [(a, a + steps) for a in range(max(0, -steps), min(count, count - steps))]
    return lax.ppermute(value, axis, pairs)


def swapped(value, axis, mask):
    count = lax.axis_size(axis)
    return lax.ppermute(value, axis, [(a, a ^ mask) for a in range(count)])


def chip_meta(meta):
    first, second, end, core = meta[0], meta[1], meta[2], meta[3]
    return first, second - first, end - first, core


def place(meta, index):
    _, low, _, core = chip_meta(meta)
    on_second = (index >= low).astype(jnp.int32)
    slot = jnp.clip(index - on_second * low, 0, 3)
    return on_second == core, slot


SMEM = pl.BlockSpec(memory_space=pltpu.SMEM)
VMEM = pl.BlockSpec(memory_space=pltpu.VMEM)


def prep_body(meta, gate, cot, x, cot_all, w_out, send, cot_out, w_other, sems):
    slots, rows, half = w_other.shape
    step = pl.program_id(0)
    other = pl.ds(pl.multiple_of((1 - meta[3]) * half, half), half)
    copies = [
        pltpu.make_async_copy(x.at[:, :, other], send.at[0], sems.at[0]),
        pltpu.make_async_copy(cot_all.at[:, :, other], cot_out, sems.at[1]),
    ]

    @pl.when(step == 0)
    def _():
        for copy in copies:
            copy.start()

    w_out[0] = (gate[0].astype(F32) * cot[0].astype(F32)).astype(BF)
    w_other[step] = w_out[0, :, other]
    pltpu.make_async_copy(w_other.at[step], send.at[1, step], sems.at[2 + step]).start()

    @pl.when(step == slots - 1)
    def _():
        for copy in copies:
            copy.wait()
        for s in range(slots):
            pltpu.make_async_copy(w_other.at[s], send.at[1, s], sems.at[2 + s]).wait()


def prep(meta, gate, cot, x):
    slots, rows, width = x.shape
    half = width // 2
    full = pl.BlockSpec((1, rows, width), lambda s, m: (s, 0, 0))
    loose = pl.BlockSpec(memory_space=pl.ANY)
    return pl.pallas_call(
        prep_body,
        grid_spec=pltpu.PrefetchScalarGridSpec(
            num_scalar_prefetch=1,
            grid=(slots,),
            in_specs=[full, full, loose, loose],
            out_specs=[full, loose, loose],
            scratch_shapes=[
                pltpu.VMEM((slots, rows, half), BF),
                pltpu.SemaphoreType.DMA((2 + slots,)),
            ],
        ),
        out_shape=[
            jax.ShapeDtypeStruct(x.shape, BF),
            jax.ShapeDtypeStruct((2, slots, rows, half), BF),
            jax.ShapeDtypeStruct((slots, rows, half), BF),
        ],
        compiler_params=params(),
        cost_estimate=pl.CostEstimate(flops=2 << 20, bytes_accessed=12 << 20, transcendentals=0),
        name="prep",
    )(meta, gate, cot, x, cot)


def pack_body(tiles, x_at, w_at, halos, meta, x, w, theirs, *rest):
    x_halos, w_halos = rest[:halos], rest[halos : 2 * halos]
    x_out, w_out, sems = rest[2 * halos :]
    half = x_out.shape[2]
    _, _, count, core = chip_meta(meta)
    lanes = pl.ds(pl.multiple_of(core * half, half), half)
    for which, (own, out) in enumerate(((x, x_out), (w, w_out))):
        for j in range(tiles):
            sem = sems.at[which * tiles + j]
            index = (x_at if which == 0 else w_at)(j, count)
            mine, slot = place(meta, index)
            depth = -1 - index if which == 0 else index - count
            here = depth < 0

            @pl.when(here & mine)
            def _():
                pltpu.make_async_copy(own.at[slot, :, lanes], out.at[j], sem).start()

            @pl.when(here & jnp.logical_not(mine))
            def _():
                pltpu.make_async_copy(theirs.at[which, slot], out.at[j], sem).start()

            for h in range(halos):
                halo = (x_halos if which == 0 else w_halos)[h]
                inside = jnp.clip(depth - h * PIECE, 0, PIECE - 1)
                row = PIECE - 1 - inside if which == 0 else inside

                @pl.when((depth >= h * PIECE) & (depth < (h + 1) * PIECE))
                def _():
                    pltpu.make_async_copy(halo.at[row], out.at[j], sem).start()

    for which, out in enumerate((x_out, w_out)):
        for j in range(tiles):
            pltpu.make_async_copy(theirs.at[which, 0], out.at[j], sems.at[which * tiles + j]).wait()


def pack(meta, x, w, theirs, tiles, x_at, w_at, x_halos=(), w_halos=()):
    slots, rows, width = x.shape
    half = width // 2
    halos = len(x_halos)
    loose = pl.BlockSpec(memory_space=pl.ANY)
    return pl.pallas_call(
        functools.partial(pack_body, tiles, x_at, w_at, halos),
        grid_spec=pltpu.PrefetchScalarGridSpec(
            num_scalar_prefetch=1,
            grid=(1,),
            in_specs=[loose] * (3 + 2 * halos),
            out_specs=[loose, loose],
            scratch_shapes=[pltpu.SemaphoreType.DMA((2 * tiles,))],
        ),
        out_shape=[jax.ShapeDtypeStruct((tiles, rows, half), BF)] * 2,
        compiler_params=params(),
        cost_estimate=pl.CostEstimate(flops=0, bytes_accessed=tiles << 20, transcendentals=0),
        name="pack",
    )(meta, x, w, theirs, *x_halos, *w_halos)


def readers_of(table, tile, total):
    live = (tile >= 0) & (tile < total)
    return jnp.where(live, table[total + jnp.clip(tile, 0, total - 1)], 0)


def sources_of(table, tile, total):
    return table[jnp.clip(tile, 0, total - 1)]


def kept(live, tile):
    return jnp.where(live, tile, jnp.zeros_like(tile))


def dot(a, b):
    return jnp.dot(a, b, preferred_element_type=F32)


def reversal(rows):
    r = lax.broadcasted_iota(jnp.int32, (rows, rows), 0)
    c = lax.broadcasted_iota(jnp.int32, (rows, rows), 1)
    return jnp.where(r + c == rows - 1, 1.0, 0.0).astype(BF)


def diagonal_sums(square):
    rows, width = square.shape
    padded = jnp.concatenate([square, jnp.zeros((rows, rows), F32)], axis=1)
    skewed = pltpu.roll(padded, 0, 1, stride=1, stride_axis=0)
    total = jnp.sum(skewed, axis=0, keepdims=True)
    total = pltpu.roll(jnp.broadcast_to(total, (8, width + rows)), width + 1, 1)
    return total[:1, :width]


def lanes_of(group):
    return pl.ds(pl.multiple_of(group * GROUP, GROUP), GROUP)


def pick(mine, theirs, meta, index, group, groups):
    own, slot = place(meta, index)
    return jnp.where(own, mine[slot, :, lanes_of(meta[3] * groups + group)], theirs[slot, :, lanes_of(group)])


def band(row, shift):
    rows, width = GROUP, row.shape[1]
    spread = jnp.broadcast_to(jnp.concatenate([row, jnp.zeros((1, rows), F32)], axis=1), (rows, width + rows))
    return pltpu.roll(spread, shift, 1, stride=1, stride_axis=0)[:, :width].astype(BF)


def own_body(lags, total, base, steps, groups, meta, table, filt, x, theirs, w,
             conv_out, adj_out, fwd_out, bwd_out, sums_out, flip, xs, xl, ws, turned):
    cap, rows, _ = xs.shape
    first, _, count, _ = chip_meta(meta)
    width = filt.shape[1]
    ahead = [jnp.minimum(readers_of(table, first + s, total), count - s) for s in range(cap)]
    behind = [sources_of(table, first + i, total) for i in range(cap)]
    mine = filt[pl.ds(pl.multiple_of(meta[3] * groups, groups), groups), :].astype(BF)
    for k in range(lags):
        block = mine[:, (lags - 1 - k) * rows : (lags - k) * rows]
        flip[:, k * rows : (k + 1) * rows] = dot(block, reversal(rows))

    def one(step, carry):
        group = base + step
        row = pl.ds(meta[3] * groups + group, 1)
        bwd_out[step] = band(filt[row, :].astype(BF).astype(F32), 0)
        fwd_out[step] = band(flip[pl.ds(group, 1), :], width + 1)
        for s in range(cap):
            tile = pick(x, theirs.at[0], meta, s, group, groups)
            xs[s] = tile
            xl[:, s * rows : (s + 1) * rows] = tile
            tile = pick(w, theirs.at[1], meta, s, group, groups)
            ws[s] = tile
            turned[s] = tile.T
        lanes = lanes_of(step)
        for i in range(cap):
            right = jnp.concatenate([kept(i - s < behind[i], xs[s]) for s in range(i + 1)], axis=0)
            conv_out[i, :, lanes] = dot(fwd_out[step, :, (lags - 1 - i) * rows :], right)
        for s in range(cap):
            right = jnp.concatenate([kept(k < ahead[s], ws[s + k]) for k in range(cap - s)], axis=0)
            adj_out[s, :, lanes] = dot(bwd_out[step, :, : (cap - s) * rows], right)
        back = dot(reversal(rows), xl[...]).astype(BF)
        squares = []
        for k in range(0, lags, 2):
            right = [
                [kept(q < ahead[s], turned[s + q]) if s + q < cap else jnp.zeros((GROUP, rows), BF) for q in (k, k + 1)]
                for s in range(cap - k)
            ]
            right = jnp.concatenate([jnp.concatenate(pair, axis=1) for pair in right], axis=0)
            squares.append(dot(back[:, : (cap - k) * rows], right))
        sums_out[pl.ds(step, 1), :] = diagonal_sums(jnp.concatenate(squares, axis=1))
        return carry

    lax.fori_loop(0, steps, one, 0)


def own_pairs(meta, table, filt, x, w, theirs, lags, base, steps):
    slots, rows, width = x.shape
    groups = width // 2 // GROUP
    taps = filt.shape[1]
    cap = 2 * slots
    return pl.pallas_call(
        functools.partial(own_body, lags, table.shape[0] // 2, base, steps, groups),
        in_specs=[SMEM, SMEM] + [VMEM] * 4,
        out_specs=[VMEM] * 5,
        scratch_shapes=[
            pltpu.VMEM((groups, taps), F32),
            pltpu.VMEM((cap, rows, GROUP), BF),
            pltpu.VMEM((rows, cap * GROUP), BF),
            pltpu.VMEM((cap, rows, GROUP), BF),
            pltpu.VMEM((cap, GROUP, rows), BF),
        ],
        out_shape=[
            jax.ShapeDtypeStruct((cap, rows, steps * GROUP), F32),
            jax.ShapeDtypeStruct((cap, rows, steps * GROUP), F32),
            jax.ShapeDtypeStruct((steps, rows, taps), BF),
            jax.ShapeDtypeStruct((steps, rows, taps), BF),
            jax.ShapeDtypeStruct((steps, taps), F32),
        ],
        compiler_params=params(),
        cost_estimate=pl.CostEstimate(flops=steps * 1_000_000_000, bytes_accessed=steps << 20, transcendentals=0),
        name="own_pairs",
    )(meta, table, filt, x, theirs, w)


def cross_body(lags, total, groups, meta, table, prior, more, x, theirs, w, xn, wn,
               sums_out, xl, near, deep):
    rows = xl.shape[0]
    blocks = lags - 1
    first, _, count, _ = chip_meta(meta)
    split = blocks - NEAR
    found = []
    for p in range(blocks):
        s = p - blocks if p >= split else count - 1 - (blocks - 1 - p)
        number = readers_of(table, first + s, total)
        found.append(number if p >= split else jnp.where(s >= 0, number, 0))
    steps = prior.shape[0]
    for part in range(2):
        source = (prior, more)[part]

        def one(step, carry):
            group = part * steps + step
            lanes = lanes_of(group)
            for p in range(split):
                index = count - 1 - (blocks - 1 - p)
                xl[:, p * rows : (p + 1) * rows] = pick(x, theirs.at[0], meta, index, group, groups)
            for p in range(NEAR):
                at = split + p
                xl[:, at * rows : (at + 1) * rows] = xn[p, :, lanes]
            for t in range(blocks):
                tile = pick(w, theirs.at[1], meta, t, group, groups)
                if t >= NEAR:
                    tile = jnp.where(t < count, tile, wn[jnp.clip(t - count, 0, PIECE - 1), :, lanes])
                near[t] = tile.T
            for a in range(split):
                deep[a] = wn[a, :, lanes].T
            back = dot(reversal(rows), xl[...]).astype(BF)

            def tile_at(p, k):
                s = p - blocks
                if p >= split and s + k >= 0:
                    return kept(k < found[p], near[s + k])
                if p < split and s + k >= 0:
                    return kept(k < found[p], deep[s + k])
                return jnp.zeros((GROUP, rows), BF)

            squares = []
            for k in range(0, lags, 2):
                low = blocks - 1 - k
                right = [jnp.concatenate([tile_at(p, k), tile_at(p, k + 1)], axis=1) for p in range(low, blocks)]
                squares.append(dot(back[:, low * rows :], jnp.concatenate(right, axis=0)))
            total_sum = diagonal_sums(jnp.concatenate(squares, axis=1))
            sums_out[pl.ds(group, 1), :] = source[pl.ds(step, 1), :] + total_sum
            return carry

        lax.fori_loop(0, steps, one, 0)


def cross_squares(meta, table, prior, more, x, w, theirs, x_halo, w_halo, lags):
    slots, rows, width = x.shape
    groups = width // 2 // GROUP
    taps = prior.shape[1]
    blocks = lags - 1
    return pl.pallas_call(
        functools.partial(cross_body, lags, table.shape[0] // 2, groups),
        in_specs=[SMEM, SMEM] + [VMEM] * 7,
        out_specs=VMEM,
        scratch_shapes=[
            pltpu.VMEM((rows, blocks * GROUP), BF),
            pltpu.VMEM((blocks, GROUP, rows), BF),
            pltpu.VMEM((blocks - NEAR, GROUP, rows), BF),
        ],
        out_shape=jax.ShapeDtypeStruct((groups, taps), F32),
        compiler_params=params(),
        cost_estimate=pl.CostEstimate(flops=3_000_000_000, bytes_accessed=6 << 20, transcendentals=0),
        name="cross_squares",
    )(meta, table, prior, more, x, theirs, w, x_halo, w_halo)


def near_body(lags, total, groups, meta, table, conv_a, conv_b, adj_a, adj_b, fwd_a, fwd_b, bwd_a, bwd_b,
              xn, wn, cot, cot_t, gate_out, input_out, send_out, conv_out, adj_out, accum):
    slots, rows, _ = gate_out.shape
    cap = 2 * slots
    first, low, count, core = chip_meta(meta)
    high = count - low
    blocks = lags - 1
    behind = [sources_of(table, first + i, total) for i in range(blocks)]
    ahead = [readers_of(table, first + count - 1 - c, total) for c in range(blocks)]
    steps = fwd_a.shape[0]
    for part in range(2):
        conv, adj, fwd, bwd = ((conv_a, adj_a, fwd_a, bwd_a), (conv_b, adj_b, fwd_b, bwd_b))[part]

        def one(step, carry):
            group = part * steps + step
            lanes, local = lanes_of(group), lanes_of(step)
            xs = [xn[p, :, lanes] for p in range(NEAR)]
            ws = [wn[p, :, lanes] for p in range(NEAR)]
            for i in range(blocks):
                farthest = min(blocks, i + NEAR)
                start = (blocks - farthest) * rows
                size = (farthest - i) * rows
                right = [kept(lag < behind[i], xs[i + NEAR - lag]) for lag in range(farthest, i, -1)]
                term = dot(fwd[step, :, start : start + size], jnp.concatenate(right, axis=0))
                accum[i] = conv[i, :, local] + term
            accum[blocks] = conv[blocks, :, local]
            for i in range(blocks - NEAR):
                conv_out[i, :, lanes] = accum[i]
            for c in range(blocks):
                tiles = min(NEAR, blocks - c)
                start = (c + 1) * rows
                right = jnp.concatenate([kept(c + 1 + a < ahead[c], ws[a]) for a in range(tiles)], axis=0)
                term = dot(bwd[step, :, start : start + tiles * rows], right)
                accum[cap + blocks + count - 1 - c] = term
            for c in range(blocks, cap):
                accum[cap + blocks + count - 1 - c] = jnp.zeros((rows, GROUP), F32)
            for c in range(blocks - NEAR):
                at = count - 1 - c
                adj_out[c, :, lanes] = adj[at, :, local] + accum[cap + blocks + at]
            for slot in range(slots):
                for own in (True, False):
                    second = core if own else 1 - core
                    index = jnp.minimum(slot + second * low, cap - 1)
                    live = slot < jnp.where(second == 1, high, low)
                    cot_tile = cot[slot, :, lanes_of(core * groups + group)] if own else cot_t[slot, :, lanes]
                    grad = jnp.where(live, cot_tile.astype(F32) * accum[index], 0.0).astype(BF)
                    sum_ = adj[index, :, local] + accum[cap + blocks + index]
                    back = jnp.where(live, sum_, 0.0).astype(BF)
                    if own:
                        gate_out[slot, :, lanes] = grad
                        input_out[slot, :, lanes] = back
                    else:
                        send_out[0, slot, :, lanes] = grad
                        send_out[1, slot, :, lanes] = back
            return carry

        lax.fori_loop(0, steps, one, 0)


def near_pairs(meta, table, one, two, x_halo, w_halo, cot, cot_theirs, lags):
    slots, rows, width = cot.shape
    half = width // 2
    far = lags - 1 - NEAR
    pieces = [value for pair in zip(one, two) for value in pair]
    return pl.pallas_call(
        functools.partial(near_body, lags, table.shape[0] // 2, half // GROUP),
        in_specs=[SMEM, SMEM] + [VMEM] * 12,
        out_specs=[VMEM] * 5,
        scratch_shapes=[
            pltpu.VMEM((4 * slots + lags - 1, rows, GROUP), F32),
        ],
        out_shape=[
            jax.ShapeDtypeStruct((slots, rows, half), BF),
            jax.ShapeDtypeStruct((slots, rows, half), BF),
            jax.ShapeDtypeStruct((2, slots, rows, half), BF),
            jax.ShapeDtypeStruct((far, rows, half), F32),
            jax.ShapeDtypeStruct((far, rows, half), F32),
        ],
        compiler_params=params(),
        cost_estimate=pl.CostEstimate(flops=3_000_000_000, bytes_accessed=8 << 20, transcendentals=0),
        name="near_pairs",
    )(meta, table, *pieces, x_halo, w_halo, cot, cot_theirs)


def far_body(lags, total, groups, meta, table, conv, adj, fwd_a, fwd_b, bwd_a, bwd_b, xf, wf, cot, cot_t,
             gate_in, input_in, send_in, gate_out, input_out, send_out):
    far, rows, _ = xf.shape
    first, _, count, _ = chip_meta(meta)
    behind = [sources_of(table, first + i, total) for i in range(far)]
    ahead = [readers_of(table, first + count - 1 - c, total) for c in range(far)]
    steps = fwd_a.shape[0]
    for part in range(2):
        fwd, bwd = ((fwd_a, bwd_a), (fwd_b, bwd_b))[part]

        def one(step, carry):
            group = part * steps + step
            lanes = lanes_of(group)
            xs = [xf[p, :, lanes] for p in range(far)]
            ws = [wf[p, :, lanes] for p in range(far)]
            results = []
            for i in range(far):
                right = [kept(lags - 1 + i - p < behind[i], xs[p]) for p in range(i, far)]
                term = dot(fwd[step, :, : (far - i) * rows], jnp.concatenate(right, axis=0))
                value = pick(cot, cot_t, meta, i, group, groups).astype(F32) * (conv[i, :, lanes] + term)
                results.append((i, gate_out, 0, value.astype(BF)))
            for c in range(far):
                right = [kept(c + NEAR + 1 + a < ahead[c], ws[a]) for a in range(far - c)]
                term = dot(bwd[step, :, (c + NEAR + 1) * rows :], jnp.concatenate(right, axis=0))
                results.append((count - 1 - c, input_out, 1, (adj[c, :, lanes] + term).astype(BF)))
            for index, out, which, value in results:
                mine, slot = place(meta, index)

                @pl.when(mine)
                def _():
                    out[slot, :, lanes] = value

                @pl.when(jnp.logical_not(mine))
                def _():
                    send_out[which, slot, :, lanes] = value

            return carry

        lax.fori_loop(0, steps, one, 0)


def far_pairs(meta, table, conv, adj, one, two, x_halo, w_halo, cot, cot_theirs, gate, inp, send, lags):
    width = cot.shape[2]
    pieces = [one[2], two[2], one[3], two[3]]
    return pl.pallas_call(
        functools.partial(far_body, lags, table.shape[0] // 2, width // 2 // GROUP),
        in_specs=[SMEM, SMEM] + [VMEM] * 13,
        out_specs=[VMEM] * 3,
        out_shape=[
            jax.ShapeDtypeStruct(gate.shape, BF),
            jax.ShapeDtypeStruct(inp.shape, BF),
            jax.ShapeDtypeStruct(send.shape, BF),
        ],
        input_output_aliases={12: 0, 13: 1, 14: 2},
        compiler_params=params(),
        cost_estimate=pl.CostEstimate(flops=800_000_000, bytes_accessed=4 << 20, transcendentals=0),
        name="far_pairs",
    )(meta, table, conv, adj, *pieces, x_halo, w_halo, cot, cot_theirs, gate, inp, send)


def settle_body(mine, meta, gate, inp, gate_in, input_in, gate_out, input_out, sems):
    slots, _, half = gate.shape
    core = meta[3] if mine else 1 - meta[3]
    lanes = pl.ds(pl.multiple_of(core * half, half), half)
    copies = []
    for which, (source, out) in enumerate(((gate, gate_out), (inp, input_out))):
        for s in range(slots):
            copies.append(pltpu.make_async_copy(source.at[s], out.at[s, :, lanes], sems.at[which * slots + s]))
    for copy in copies:
        copy.start()
    for copy in copies:
        copy.wait()


def place_mine(meta, gate, inp):
    slots, rows, half = gate.shape

    def body(meta, gate, inp, gate_out, input_out, sems):
        settle_body(True, meta, gate, inp, None, None, gate_out, input_out, sems)

    loose = pl.BlockSpec(memory_space=pl.ANY)
    return pl.pallas_call(
        body,
        in_specs=[SMEM, VMEM, VMEM],
        out_specs=[loose, loose],
        scratch_shapes=[pltpu.SemaphoreType.DMA((2 * slots,))],
        out_shape=[jax.ShapeDtypeStruct((slots, rows, 2 * half), BF)] * 2,
        compiler_params=params(),
        name="place_mine",
    )(meta, gate, inp)


def join(meta, got, gate, inp):
    slots = gate.shape[0]

    def body(meta, got, gate_in, input_in, gate_out, input_out, sems):
        settle_body(False, meta, got.at[0], got.at[1], gate_in, input_in, gate_out, input_out, sems)

    loose = pl.BlockSpec(memory_space=pl.ANY)
    return pl.pallas_call(
        body,
        in_specs=[SMEM, VMEM, loose, loose],
        out_specs=[loose, loose],
        scratch_shapes=[pltpu.SemaphoreType.DMA((2 * slots,))],
        out_shape=[jax.ShapeDtypeStruct(gate.shape, BF)] * 2,
        input_output_aliases={2: 0, 3: 1},
        compiler_params=params(),
        name="join",
    )(meta, got, gate, inp)


def per_device(conv_input, gate_signal, cotangent, filters, tile_owner, support):
    slots, rows, width = conv_input.shape
    lags = support.shape[1]
    filter_count, taps = filters.shape
    total = tile_owner.shape[0]
    tie = lax.optimization_barrier
    me = lax.axis_index("ctx")
    core = me % 2
    entry = jnp.arange(8, dtype=jnp.int32)
    before = jnp.sum((tile_owner[None, :] < (me - core + entry)[:, None]).astype(jnp.int32), axis=1)
    meta = jnp.where(entry == 3, core, before)

    behind = jnp.sum((support >= 0).astype(jnp.int32), axis=1)
    ahead = sum(jnp.pad((behind[k:] > k).astype(jnp.int32), (0, k)) for k in range(lags))
    table = jnp.concatenate([behind, ahead])
    meta, table = tie((meta, table))

    def up(value):
        return shifted(value, "ctx", 2)

    def down(value):
        return shifted(value, "ctx", -2)

    w, send, cot_send = prep(meta, gate_signal, cotangent, conv_input)
    theirs = swapped(send, "ctx", 1)
    x = conv_input
    xs, ws = pack(meta, x, w, theirs, PIECE, lambda j, n: n - PIECE + j, lambda j, n: j)
    x0, w0 = up(xs), down(ws)
    cot_theirs = swapped(cot_send, "ctx", 1)
    half_groups = width // 2 // GROUP // 2
    one = own_pairs(meta, table, filters, x, w, theirs, lags, 0, half_groups)
    two = own_pairs(meta, table, filters, x, w, theirs, lags, half_groups, half_groups)
    x0, w0, one, two = tie((x0, w0, one, two))
    *one, first_sums = one
    *two, second_sums = two
    sums = cross_squares(meta, table, first_sums, second_sums, x, w, theirs, x0, w0, lags)

    def stage(sums, axis, masks, filler):
        moved = [swapped(sums, axis, mask) for mask in masks]
        out = filler(tie((sums, meta))[1])
        total_sum = sums + moved[0]
        if len(masks) == 3:
            total_sum = total_sum + (moved[1] + moved[2])
        return tie((total_sum, out))

    def relay(meta):
        return pack(
            meta, x, w, theirs, lags - 1 - NEAR, lambda j, n: n - lags + 1 + j, lambda j, n: NEAR + j, (x0,), (w0,)
        )

    def close(meta):
        return near_pairs(meta, table, one, two, x0, w0, cotangent, cot_theirs, lags)

    sums, (xs, ws) = stage(sums, "ctx", (2, 4, 6), relay)
    x2, w2 = up(xs), down(ws)
    sums, (gate, inp, back, conv, adj) = stage(sums, "ch", (1, 2, 3), close)

    def finish(meta):
        return far_pairs(
            meta, table, conv, adj, one, two, x2, w2, cotangent, cot_theirs, gate, inp, back, lags
        )

    sums, (gate, inp, back) = stage(sums, "ctx", (8, 16, 24), finish)
    got = swapped(back, "ctx", 1)
    sums, (gate, inp) = stage(sums, "ctx", (32,), lambda meta: place_mine(meta, gate, inp))
    norm = 1.0 / math.sqrt(total * rows * width * lax.axis_size("ch") / filter_count)
    sums = sums * norm
    partner = swapped(sums, "ctx", 1)
    gate, inp = join(tie((sums, meta))[1], got, gate, inp)
    partner, gate, inp = tie((partner, gate, inp))
    low = jnp.where(core == 0, sums, partner)
    high = jnp.where(core == 0, partner, sums)
    return gate, inp, jnp.concatenate([low, high], axis=0)


def solution(mesh):
    return jax.shard_map(
        per_device,
        mesh=mesh,
        in_specs=(P("ctx", None, "ch"), P("ctx", None, "ch"), P("ctx", None, "ch"), P(), P(), P()),
        out_specs=(P("ctx", None, "ch"), P("ctx", None, "ch"), P()),
        check_vma=False,
    )
```

```python
import functools
import math

import jax
import jax.numpy as jnp
from jax import lax
from jax.experimental import pallas as pl
from jax.experimental.pallas import tpu as pltpu
from jax.sharding import PartitionSpec as P

GROUP = 128
NEAR = 4
PIECE = 4
BF = jnp.bfloat16
F32 = jnp.float32
VMEM_LIMIT = 8 * 1024 * 1024
LEAD_LIMIT = 56 * 1024 * 1024
REST_LIMIT = 50 * 1024 * 1024


def params(limit=VMEM_LIMIT):
    return pltpu.CompilerParams(vmem_limit_bytes=limit)


def shifted(value, axis, steps):
    count = lax.axis_size(axis)
    pairs = [(a, a + steps) for a in range(max(0, -steps), min(count, count - steps))]
    return lax.ppermute(value, axis, pairs)


def swapped(value, axis, mask):
    count = lax.axis_size(axis)
    return lax.ppermute(value, axis, [(a, a ^ mask) for a in range(count)])


def chip_meta(meta):
    first, second, end, core = meta[0], meta[1], meta[2], meta[3]
    return first, second - first, end - first, core


def place(meta, index):
    _, low, _, core = chip_meta(meta)
    on_second = (index >= low).astype(jnp.int32)
    slot = jnp.clip(index - on_second * low, 0, 3)
    return on_second == core, slot


SMEM = pl.BlockSpec(memory_space=pltpu.SMEM)
VMEM = pl.BlockSpec(memory_space=pltpu.VMEM)


HBM = pl.BlockSpec(memory_space=pltpu.HBM)


def lower_bound(owner, value):
    low, high = jnp.int32(0), jnp.int32(owner.shape[0])
    for _ in range(owner.shape[0].bit_length()):
        middle = jnp.minimum((low + high) // 2, owner.shape[0] - 1)
        below = (owner[middle] < value) & (low < high)
        low, high = jnp.where(below, middle + 1, low), jnp.where(below, high, jnp.minimum(high, middle))
    return low


def halves_body(mine, me, gate, cot, x, x_out, cot_out, gates, sems):
    slots, _, half = gates.shape
    core = me % 2 if mine else 1 - me % 2
    lanes = pl.ds(pl.multiple_of(core * half, half), half)
    copies = []
    for which, (source, target) in enumerate(((gate, gates), (cot, cot_out), (x, x_out))):
        copies.append(
            [pltpu.make_async_copy(source.at[s, :, lanes], target.at[s], sems.at[which * slots + s]) for s in range(slots)]
        )
    for s in range(slots):
        copies[0][s].start()
        copies[1][s].start()
    for s in range(slots):
        copies[2][s].start()
    return copies


def product_body(copies, gates, cot_out, w_out):
    for s in range(gates.shape[0]):
        copies[0][s].wait()
        copies[1][s].wait()
        w_out[s] = (gates[s].astype(F32) * cot_out[s].astype(F32)).astype(BF)
    for copy in copies[2]:
        copy.wait()


def lead_body(me, owner, gate, cot, x, send, meta, gates, cots, sems):
    copies = halves_body(False, me[0], gate, cot, x, send.at[0], cots, gates, sems)
    core = me[0] % 2
    base = me[0] - core
    for i in range(3):
        meta[i] = lower_bound(owner, base + i)
    meta[3] = core
    for i in range(4, 8):
        meta[i] = 0
    product_body(copies, gates, cots, send.at[1])


def lead(me, owner, gate, cot, x):
    slots, rows, width = x.shape
    half = width // 2
    return pl.pallas_call(
        lead_body,
        in_specs=[SMEM, SMEM, HBM, HBM, HBM],
        out_specs=[VMEM, SMEM],
        scratch_shapes=[pltpu.VMEM((slots, rows, half), BF)] * 2 + [pltpu.SemaphoreType.DMA((3 * slots,))],
        out_shape=[
            jax.ShapeDtypeStruct((2, slots, rows, half), BF),
            jax.ShapeDtypeStruct((8,), jnp.int32),
        ],
        compiler_params=params(LEAD_LIMIT),
        cost_estimate=pl.CostEstimate(flops=1 << 20, bytes_accessed=6 << 20, transcendentals=0),
        name="lead",
    )(me, owner, gate, cot, x)


READS = 16


def rest_body(meta, support, gate, cot, x, x_out, w_out, cot_out, cot_send, reach, gates, sems):
    copies = halves_body(True, meta[3], gate, cot, x, x_out, cot_out, gates, sems)
    slots, _, half = gates.shape
    other = pl.ds(pl.multiple_of((1 - meta[3]) * half, half), half)
    extra = [
        pltpu.make_async_copy(cot.at[s, :, other], cot_send.at[s], sems.at[3 * slots + s]) for s in range(slots)
    ]
    for copy in extra:
        copy.start()
    lags, total = support.shape
    first = meta[0]
    cap = 2 * gates.shape[0]
    for s in range(-NEAR, cap):
        tile = first + s
        found = jnp.int32(0)
        for lag in range(lags):
            at = jnp.clip(tile + lag, 0, total - 1)
            found += ((tile >= 0) & (tile + lag < total) & (support[lag, at] >= 0)).astype(jnp.int32)
        reach[s + NEAR] = found
    for i in range(cap):
        at = jnp.clip(first + i, 0, total - 1)
        found = jnp.int32(0)
        for lag in range(lags):
            found += (support[lag, at] >= 0).astype(jnp.int32)
        reach[READS + i] = found
    for i in range(NEAR + cap, READS):
        reach[i] = 0
    for i in range(READS + cap, 2 * READS):
        reach[i] = 0
    product_body(copies, gates, cot_out, w_out)
    for copy in extra:
        copy.wait()


def rest(meta, support, gate, cot, x):
    slots, rows, width = x.shape
    half = width // 2
    return pl.pallas_call(
        rest_body,
        in_specs=[SMEM, SMEM, HBM, HBM, HBM],
        out_specs=[VMEM, VMEM, VMEM, VMEM, SMEM],
        scratch_shapes=[pltpu.VMEM((slots, rows, half), BF), pltpu.SemaphoreType.DMA((4 * slots,))],
        out_shape=[jax.ShapeDtypeStruct((slots, rows, half), BF)] * 4
        + [jax.ShapeDtypeStruct((2 * READS,), jnp.int32)],
        compiler_params=params(REST_LIMIT),
        cost_estimate=pl.CostEstimate(flops=1 << 20, bytes_accessed=6 << 20, transcendentals=0),
        name="rest",
    )(meta, support, gate, cot, x)


def pack_body(tiles, x_at, w_at, halos, meta, x, w, theirs, *rest):
    x_halos, w_halos = rest[:halos], rest[halos : 2 * halos]
    x_out, w_out, sems = rest[2 * halos :]
    _, _, count, _ = chip_meta(meta)
    for which, (own, out) in enumerate(((x, x_out), (w, w_out))):
        for j in range(tiles):
            sem = sems.at[which * tiles + j]
            index = (x_at if which == 0 else w_at)(j, count)
            mine, slot = place(meta, index)
            depth = -1 - index if which == 0 else index - count
            here = depth < 0

            @pl.when(here & mine)
            def _():
                pltpu.make_async_copy(own.at[slot], out.at[j], sem).start()

            @pl.when(here & jnp.logical_not(mine))
            def _():
                pltpu.make_async_copy(theirs.at[which, slot], out.at[j], sem).start()

            for h in range(halos):
                halo = (x_halos if which == 0 else w_halos)[h]
                inside = jnp.clip(depth - h * PIECE, 0, PIECE - 1)
                row = PIECE - 1 - inside if which == 0 else inside

                @pl.when((depth >= h * PIECE) & (depth < (h + 1) * PIECE))
                def _():
                    pltpu.make_async_copy(halo.at[row], out.at[j], sem).start()

    for which, out in enumerate((x_out, w_out)):
        for j in range(tiles):
            pltpu.make_async_copy(theirs.at[which, 0], out.at[j], sems.at[which * tiles + j]).wait()


def pack(meta, x, w, theirs, tiles, x_at, w_at, x_halos=(), w_halos=()):
    _, rows, half = x.shape
    halos = len(x_halos)
    loose = pl.BlockSpec(memory_space=pl.ANY)
    return pl.pallas_call(
        functools.partial(pack_body, tiles, x_at, w_at, halos),
        in_specs=[SMEM] + [loose] * (3 + 2 * halos),
        out_specs=[loose, loose],
        scratch_shapes=[pltpu.SemaphoreType.DMA((2 * tiles,))],
        out_shape=[jax.ShapeDtypeStruct((tiles, rows, half), BF)] * 2,
        compiler_params=params(),
        cost_estimate=pl.CostEstimate(flops=0, bytes_accessed=tiles << 20, transcendentals=0),
        name="pack",
    )(meta, x, w, theirs, *x_halos, *w_halos)


def kept(live, tile):
    return jnp.where(live, tile, jnp.zeros_like(tile))


def dot(a, b):
    return jnp.dot(a, b, preferred_element_type=F32)


def reversal(rows):
    r = lax.broadcasted_iota(jnp.int32, (rows, rows), 0)
    c = lax.broadcasted_iota(jnp.int32, (rows, rows), 1)
    return jnp.where(r + c == rows - 1, 1.0, 0.0).astype(BF)


def diagonal_sums(square):
    rows, width = square.shape
    padded = jnp.concatenate([square, jnp.zeros((rows, rows), F32)], axis=1)
    skewed = pltpu.roll(padded, 0, 1, stride=1, stride_axis=0)
    total = jnp.sum(skewed, axis=0, keepdims=True)
    total = pltpu.roll(jnp.broadcast_to(total, (8, width + rows)), width + 1, 1)
    return total[:1, :width]


def lanes_of(group):
    return pl.ds(pl.multiple_of(group * GROUP, GROUP), GROUP)


def pick(mine, theirs, meta, index, group):
    own, slot = place(meta, index)
    return jnp.where(own, mine[slot, :, lanes_of(group)], theirs[slot, :, lanes_of(group)])


def band(row, shift):
    rows, width = GROUP, row.shape[1]
    spread = jnp.broadcast_to(jnp.concatenate([row, jnp.zeros((1, rows), F32)], axis=1), (rows, width + rows))
    return pltpu.roll(spread, shift, 1, stride=1, stride_axis=0)[:, :width].astype(BF)


def own_body(lags, base, steps, groups, meta, reach, filt, x, theirs, w,
             conv_out, adj_out, fwd_out, bwd_out, sums_out, flip, xs, xl, ws, turned):
    cap, rows, _ = xs.shape
    _, _, count, _ = chip_meta(meta)
    width = filt.shape[1]
    ahead = [jnp.minimum(reach[s + NEAR], count - s) for s in range(cap)]
    behind = [reach[READS + i] for i in range(cap)]
    mine = filt[pl.ds(pl.multiple_of(meta[3] * groups, groups), groups), :].astype(BF)
    for k in range(lags):
        block = mine[:, (lags - 1 - k) * rows : (lags - k) * rows]
        flip[:, k * rows : (k + 1) * rows] = dot(block, reversal(rows))

    def one(step, carry):
        group = base + step
        row = pl.ds(meta[3] * groups + group, 1)
        bwd_out[step] = band(filt[row, :].astype(BF).astype(F32), 0)
        fwd_out[step] = band(flip[pl.ds(group, 1), :], width + 1)
        for s in range(cap):
            tile = pick(x, theirs.at[0], meta, s, group)
            xs[s] = tile
            xl[:, s * rows : (s + 1) * rows] = tile
            tile = pick(w, theirs.at[1], meta, s, group)
            ws[s] = tile
            turned[s] = tile.T
        lanes = lanes_of(step)
        for i in range(cap):
            right = jnp.concatenate([kept(i - s < behind[i], xs[s]) for s in range(i + 1)], axis=0)
            conv_out[i, :, lanes] = dot(fwd_out[step, :, (lags - 1 - i) * rows :], right)
        for s in range(cap):
            right = jnp.concatenate([kept(k < ahead[s], ws[s + k]) for k in range(cap - s)], axis=0)
            adj_out[s, :, lanes] = dot(bwd_out[step, :, : (cap - s) * rows], right)
        back = dot(reversal(rows), xl[...]).astype(BF)
        squares = []
        for k in range(0, lags, 2):
            right = [
                [kept(q < ahead[s], turned[s + q]) if s + q < cap else jnp.zeros((GROUP, rows), BF) for q in (k, k + 1)]
                for s in range(cap - k)
            ]
            right = jnp.concatenate([jnp.concatenate(pair, axis=1) for pair in right], axis=0)
            squares.append(dot(back[:, : (cap - k) * rows], right))
        sums_out[pl.ds(step, 1), :] = diagonal_sums(jnp.concatenate(squares, axis=1))
        return carry

    lax.fori_loop(0, steps, one, 0)


def own_pairs(meta, reach, filt, x, w, theirs, lags, base, steps):
    slots, rows, half = x.shape
    groups = half // GROUP
    taps = filt.shape[1]
    cap = 2 * slots
    return pl.pallas_call(
        functools.partial(own_body, lags, base, steps, groups),
        in_specs=[SMEM, SMEM] + [VMEM] * 4,
        out_specs=[VMEM] * 5,
        scratch_shapes=[
            pltpu.VMEM((groups, taps), F32),
            pltpu.VMEM((cap, rows, GROUP), BF),
            pltpu.VMEM((rows, cap * GROUP), BF),
            pltpu.VMEM((cap, rows, GROUP), BF),
            pltpu.VMEM((cap, GROUP, rows), BF),
        ],
        out_shape=[
            jax.ShapeDtypeStruct((cap, rows, steps * GROUP), F32),
            jax.ShapeDtypeStruct((cap, rows, steps * GROUP), F32),
            jax.ShapeDtypeStruct((steps, rows, taps), BF),
            jax.ShapeDtypeStruct((steps, rows, taps), BF),
            jax.ShapeDtypeStruct((steps, taps), F32),
        ],
        compiler_params=params(),
        cost_estimate=pl.CostEstimate(flops=steps * 1_000_000_000, bytes_accessed=steps << 20, transcendentals=0),
        name="own_pairs",
    )(meta, reach, filt, x, theirs, w)


def cross_body(lags, norm, meta, reach, prior, more, x, theirs, w, xn, wn,
               sums_out, xl, near, deep):
    rows = xl.shape[0]
    blocks = lags - 1
    _, _, count, _ = chip_meta(meta)
    split = blocks - NEAR
    found = []
    for p in range(blocks):
        s = p - blocks if p >= split else count - 1 - (blocks - 1 - p)
        number = reach[s + NEAR]
        found.append(number if p >= split else jnp.where(s >= 0, number, 0))
    steps = prior.shape[0]
    for part in range(2):
        source = (prior, more)[part]

        def one(step, carry):
            group = part * steps + step
            lanes = lanes_of(group)
            for p in range(split):
                index = count - 1 - (blocks - 1 - p)
                xl[:, p * rows : (p + 1) * rows] = pick(x, theirs.at[0], meta, index, group)
            for p in range(NEAR):
                at = split + p
                xl[:, at * rows : (at + 1) * rows] = xn[p, :, lanes]
            for t in range(blocks):
                tile = pick(w, theirs.at[1], meta, t, group)
                if t >= NEAR:
                    tile = jnp.where(t < count, tile, wn[jnp.clip(t - count, 0, PIECE - 1), :, lanes])
                near[t] = tile.T
            for a in range(split):
                deep[a] = wn[a, :, lanes].T
            back = dot(reversal(rows), xl[...]).astype(BF)

            def tile_at(p, k):
                s = p - blocks
                if p >= split and s + k >= 0:
                    return kept(k < found[p], near[s + k])
                if p < split and s + k >= 0:
                    return kept(k < found[p], deep[s + k])
                return jnp.zeros((GROUP, rows), BF)

            squares = []
            for k in range(0, lags, 2):
                low = blocks - 1 - k
                right = [jnp.concatenate([tile_at(p, k), tile_at(p, k + 1)], axis=1) for p in range(low, blocks)]
                squares.append(dot(back[:, low * rows :], jnp.concatenate(right, axis=0)))
            total_sum = diagonal_sums(jnp.concatenate(squares, axis=1))
            sums_out[pl.ds(group, 1), :] = (source[pl.ds(step, 1), :] + total_sum) * norm
            return carry

        lax.fori_loop(0, steps, one, 0, unroll=2)


def cross_squares(meta, reach, prior, more, x, w, theirs, x_halo, w_halo, lags, norm):
    slots, rows, half = x.shape
    groups = half // GROUP
    taps = prior.shape[1]
    blocks = lags - 1
    return pl.pallas_call(
        functools.partial(cross_body, lags, norm),
        in_specs=[SMEM, SMEM] + [VMEM] * 7,
        out_specs=VMEM,
        scratch_shapes=[
            pltpu.VMEM((rows, blocks * GROUP), BF),
            pltpu.VMEM((blocks, GROUP, rows), BF),
            pltpu.VMEM((blocks - NEAR, GROUP, rows), BF),
        ],
        out_shape=jax.ShapeDtypeStruct((groups, taps), F32),
        compiler_params=params(),
        cost_estimate=pl.CostEstimate(flops=3_000_000_000, bytes_accessed=6 << 20, transcendentals=0),
        name="cross_squares",
    )(meta, reach, prior, more, x, theirs, w, x_halo, w_halo)


def near_body(lags, meta, reach, conv_a, conv_b, adj_a, adj_b, fwd_a, fwd_b, bwd_a, bwd_b,
              xn, wn, cot, cot_t, gate_out, input_out, send_out, conv_out, adj_out, accum):
    slots, rows, _ = gate_out.shape
    cap = 2 * slots
    _, low, count, core = chip_meta(meta)
    high = count - low
    blocks = lags - 1
    behind = [reach[READS + i] for i in range(blocks)]
    ahead = [reach[NEAR + count - 1 - c] for c in range(blocks)]
    steps = fwd_a.shape[0]
    for part in range(2):
        conv, adj, fwd, bwd = ((conv_a, adj_a, fwd_a, bwd_a), (conv_b, adj_b, fwd_b, bwd_b))[part]

        def one(step, carry):
            group = part * steps + step
            lanes, local = lanes_of(group), lanes_of(step)
            xs = [xn[p, :, lanes] for p in range(NEAR)]
            ws = [wn[p, :, lanes] for p in range(NEAR)]
            for i in range(blocks):
                farthest = min(blocks, i + NEAR)
                start = (blocks - farthest) * rows
                size = (farthest - i) * rows
                right = [kept(lag < behind[i], xs[i + NEAR - lag]) for lag in range(farthest, i, -1)]
                term = dot(fwd[step, :, start : start + size], jnp.concatenate(right, axis=0))
                accum[i] = conv[i, :, local] + term
            accum[blocks] = conv[blocks, :, local]
            for i in range(blocks - NEAR):
                conv_out[i, :, lanes] = accum[i]
            for c in range(blocks):
                tiles = min(NEAR, blocks - c)
                start = (c + 1) * rows
                right = jnp.concatenate([kept(c + 1 + a < ahead[c], ws[a]) for a in range(tiles)], axis=0)
                term = dot(bwd[step, :, start : start + tiles * rows], right)
                accum[cap + blocks + count - 1 - c] = term
            for c in range(blocks, cap):
                accum[cap + blocks + count - 1 - c] = jnp.zeros((rows, GROUP), F32)
            for c in range(blocks - NEAR):
                at = count - 1 - c
                adj_out[c, :, lanes] = adj[at, :, local] + accum[cap + blocks + at]
            for slot in range(slots):
                for own in (True, False):
                    second = core if own else 1 - core
                    index = jnp.minimum(slot + second * low, cap - 1)
                    live = slot < jnp.where(second == 1, high, low)
                    cot_tile = (cot if own else cot_t)[slot, :, lanes]
                    grad = jnp.where(live, cot_tile.astype(F32) * accum[index], 0.0).astype(BF)
                    sum_ = adj[index, :, local] + accum[cap + blocks + index]
                    back = jnp.where(live, sum_, 0.0).astype(BF)
                    if own:
                        gate_out[slot, :, lanes] = grad
                        input_out[slot, :, lanes] = back
                    else:
                        send_out[0, slot, :, lanes] = grad
                        send_out[1, slot, :, lanes] = back
            return carry

        lax.fori_loop(0, steps, one, 0)


def near_pairs(meta, reach, one, two, x_halo, w_halo, cot, cot_theirs, lags):
    slots, rows, half = cot.shape
    far = lags - 1 - NEAR
    pieces = [value for pair in zip(one, two) for value in pair]
    return pl.pallas_call(
        functools.partial(near_body, lags),
        in_specs=[SMEM, SMEM] + [VMEM] * 12,
        out_specs=[VMEM] * 5,
        scratch_shapes=[
            pltpu.VMEM((4 * slots + lags - 1, rows, GROUP), F32),
        ],
        out_shape=[
            jax.ShapeDtypeStruct((slots, rows, half), BF),
            jax.ShapeDtypeStruct((slots, rows, half), BF),
            jax.ShapeDtypeStruct((2, slots, rows, half), BF),
            jax.ShapeDtypeStruct((far, rows, half), F32),
            jax.ShapeDtypeStruct((far, rows, half), F32),
        ],
        compiler_params=params(),
        cost_estimate=pl.CostEstimate(flops=3_000_000_000, bytes_accessed=8 << 20, transcendentals=0),
        name="near_pairs",
    )(meta, reach, *pieces, x_halo, w_halo, cot, cot_theirs)


def far_body(lags, meta, reach, conv, adj, fwd_a, fwd_b, bwd_a, bwd_b, xf, wf, cot, cot_t,
             gate_in, input_in, send_in, gate_out, input_out, send_out):
    far, rows, _ = xf.shape
    _, _, count, _ = chip_meta(meta)
    behind = [reach[READS + i] for i in range(far)]
    ahead = [reach[NEAR + count - 1 - c] for c in range(far)]
    steps = fwd_a.shape[0]
    for part in range(2):
        fwd, bwd = ((fwd_a, bwd_a), (fwd_b, bwd_b))[part]

        def one(step, carry):
            group = part * steps + step
            lanes = lanes_of(group)
            xs = [xf[p, :, lanes] for p in range(far)]
            ws = [wf[p, :, lanes] for p in range(far)]
            results = []
            for i in range(far):
                right = [kept(lags - 1 + i - p < behind[i], xs[p]) for p in range(i, far)]
                term = dot(fwd[step, :, : (far - i) * rows], jnp.concatenate(right, axis=0))
                value = pick(cot, cot_t, meta, i, group).astype(F32) * (conv[i, :, lanes] + term)
                results.append((i, gate_out, 0, value.astype(BF)))
            for c in range(far):
                right = [kept(c + NEAR + 1 + a < ahead[c], ws[a]) for a in range(far - c)]
                term = dot(bwd[step, :, (c + NEAR + 1) * rows :], jnp.concatenate(right, axis=0))
                results.append((count - 1 - c, input_out, 1, (adj[c, :, lanes] + term).astype(BF)))
            for index, out, which, value in results:
                mine, slot = place(meta, index)

                @pl.when(mine)
                def _():
                    out[slot, :, lanes] = value

                @pl.when(jnp.logical_not(mine))
                def _():
                    send_out[which, slot, :, lanes] = value

            return carry

        lax.fori_loop(0, steps, one, 0)


def far_pairs(meta, reach, conv, adj, one, two, x_halo, w_halo, cot, cot_theirs, gate, inp, send, lags):
    pieces = [one[2], two[2], one[3], two[3]]
    return pl.pallas_call(
        functools.partial(far_body, lags),
        in_specs=[SMEM, SMEM] + [VMEM] * 13,
        out_specs=[VMEM] * 3,
        out_shape=[
            jax.ShapeDtypeStruct(gate.shape, BF),
            jax.ShapeDtypeStruct(inp.shape, BF),
            jax.ShapeDtypeStruct(send.shape, BF),
        ],
        input_output_aliases={12: 0, 13: 1, 14: 2},
        compiler_params=params(),
        cost_estimate=pl.CostEstimate(flops=800_000_000, bytes_accessed=4 << 20, transcendentals=0),
        name="far_pairs",
    )(meta, reach, conv, adj, *pieces, x_halo, w_halo, cot, cot_theirs, gate, inp, send)


def settle_body(mine, meta, gate, inp, gate_in, input_in, gate_out, input_out, sems):
    slots, _, half = gate.shape
    core = meta[3] if mine else 1 - meta[3]
    lanes = pl.ds(pl.multiple_of(core * half, half), half)
    copies = []
    for which, (source, out) in enumerate(((gate, gate_out), (inp, input_out))):
        for s in range(slots):
            copies.append(pltpu.make_async_copy(source.at[s], out.at[s, :, lanes], sems.at[which * slots + s]))
    for copy in copies:
        copy.start()
    for copy in copies:
        copy.wait()


def place_mine(meta, gate, inp):
    slots, rows, half = gate.shape

    def body(meta, gate, inp, gate_out, input_out, sems):
        settle_body(True, meta, gate, inp, None, None, gate_out, input_out, sems)

    loose = pl.BlockSpec(memory_space=pl.ANY)
    return pl.pallas_call(
        body,
        in_specs=[SMEM, VMEM, VMEM],
        out_specs=[loose, loose],
        scratch_shapes=[pltpu.SemaphoreType.DMA((2 * slots,))],
        out_shape=[jax.ShapeDtypeStruct((slots, rows, 2 * half), BF)] * 2,
        compiler_params=params(),
        name="place_mine",
    )(meta, gate, inp)


def join(meta, got, gate, inp, sums, moved):
    slots = gate.shape[0]
    groups, taps = sums.shape

    def body(meta, got, gate_in, input_in, sums, pair, other, other_pair, gate_out, input_out, filter_out, sems):
        core = meta[3]
        filter_out[pl.ds(pl.multiple_of(core * groups, groups), groups), :] = sums[...] + pair[...]
        filter_out[pl.ds(pl.multiple_of((1 - core) * groups, groups), groups), :] = other[...] + other_pair[...]
        settle_body(False, meta, got.at[0], got.at[1], gate_in, input_in, gate_out, input_out, sems)

    loose = pl.BlockSpec(memory_space=pl.ANY)
    return pl.pallas_call(
        body,
        in_specs=[SMEM, VMEM, loose, loose, VMEM, VMEM, VMEM, VMEM],
        out_specs=[loose, loose, VMEM],
        scratch_shapes=[pltpu.SemaphoreType.DMA((2 * slots,))],
        out_shape=[
            jax.ShapeDtypeStruct(gate.shape, BF),
            jax.ShapeDtypeStruct(inp.shape, BF),
            jax.ShapeDtypeStruct((2 * groups, taps), F32),
        ],
        input_output_aliases={2: 0, 3: 1},
        compiler_params=params(),
        name="join",
    )(meta, got, gate, inp, sums, *moved)


def per_device(conv_input, gate_signal, cotangent, filters, tile_owner, support):
    slots, rows, width = conv_input.shape
    lags = support.shape[1]
    filter_count, taps = filters.shape
    total = tile_owner.shape[0]
    tie = lax.optimization_barrier
    me = lax.axis_index("ctx")
    core = me % 2

    def up(value):
        return shifted(value, "ctx", 2)

    def down(value):
        return shifted(value, "ctx", -2)

    norm = 1.0 / math.sqrt(total * rows * width * lax.axis_size("ch") / filter_count)
    send, meta = lead(me.reshape(1), tile_owner, gate_signal, cotangent, conv_input)
    theirs = swapped(send, "ctx", 1)
    x, w, cot, cot_send, reach = rest(meta, support.T, gate_signal, cotangent, conv_input)
    xs, ws = pack(meta, x, w, theirs, PIECE, lambda j, n: n - PIECE + j, lambda j, n: j)
    x0, w0 = up(xs), down(ws)
    cot_theirs = swapped(cot_send, "ctx", 1)
    half_groups = width // 2 // GROUP // 2
    one = own_pairs(meta, reach, filters, x, w, theirs, lags, 0, half_groups)
    two = own_pairs(meta, reach, filters, x, w, theirs, lags, half_groups, half_groups)
    x0, w0, one, two = tie((x0, w0, one, two))
    *one, first_sums = one
    *two, second_sums = two
    sums = cross_squares(meta, reach, first_sums, second_sums, x, w, theirs, x0, w0, lags, norm)

    def stage(sums, axis, masks, filler):
        moved = [swapped(sums, axis, mask) for mask in masks]
        out = filler(tie((sums, meta))[1])
        total_sum = sums + moved[0]
        if len(masks) == 3:
            total_sum = total_sum + (moved[1] + moved[2])
        return tie((total_sum, out))

    def relay(meta):
        return pack(
            meta, x, w, theirs, lags - 1 - NEAR, lambda j, n: n - lags + 1 + j, lambda j, n: NEAR + j, (x0,), (w0,)
        )

    def close(meta):
        return near_pairs(meta, reach, one, two, x0, w0, cot, cot_theirs, lags)

    sums, (xs, ws) = stage(sums, "ctx", (2, 4, 6), relay)
    x2, w2 = up(xs), down(ws)
    sums, (gate, inp, back, conv, adj) = stage(sums, "ch", (1, 2, 3), close)

    def finish(meta):
        return far_pairs(
            meta, reach, conv, adj, one, two, x2, w2, cot, cot_theirs, gate, inp, back, lags
        )

    sums, (gate, inp, back) = stage(sums, "ctx", (8, 16, 24), finish)
    got = swapped(back, "ctx", 1)
    moved = [swapped(sums, "ctx", mask) for mask in (32, 1, 33)]
    gate, inp = place_mine(tie((sums, meta))[1], gate, inp)
    return join(meta, got, gate, inp, sums, moved)


def solution(mesh):
    return jax.shard_map(
        per_device,
        mesh=mesh,
        in_specs=(P("ctx", None, "ch"), P("ctx", None, "ch"), P("ctx", None, "ch"), P(), P(), P()),
        out_specs=(P("ctx", None, "ch"), P("ctx", None, "ch"), P()),
        check_vma=False,
    )
```

```python
import functools
import math

import jax
import jax.numpy as jnp
from jax import lax
from jax.experimental import pallas as pl
from jax.experimental.pallas import tpu as pltpu
from jax.sharding import PartitionSpec as P

GROUP = 128
NEAR = 4
ABOVE = 3
BF = jnp.bfloat16
F32 = jnp.float32
VMEM_LIMIT = 8 * 1024 * 1024
LEAD_LIMIT = 56 * 1024 * 1024
REST_LIMIT = 50 * 1024 * 1024


def params(limit=VMEM_LIMIT):
    return pltpu.CompilerParams(vmem_limit_bytes=limit)


def shifted(value, axis, steps):
    count = lax.axis_size(axis)
    pairs = [(a, a + steps) for a in range(max(0, -steps), min(count, count - steps))]
    return lax.ppermute(value, axis, pairs)


def swapped(value, axis, mask):
    count = lax.axis_size(axis)
    return lax.ppermute(value, axis, [(a, a ^ mask) for a in range(count)])


def chip_meta(meta):
    first, second, end, core = meta[0], meta[1], meta[2], meta[3]
    return first, second - first, end - first, core


def place(meta, index):
    _, low, _, core = chip_meta(meta)
    on_second = (index >= low).astype(jnp.int32)
    slot = jnp.clip(index - on_second * low, 0, 3)
    return on_second == core, slot


SMEM = pl.BlockSpec(memory_space=pltpu.SMEM)
VMEM = pl.BlockSpec(memory_space=pltpu.VMEM)


HBM = pl.BlockSpec(memory_space=pltpu.HBM)


def lower_bound(owner, value):
    low, high = jnp.int32(0), jnp.int32(owner.shape[0])
    for _ in range(owner.shape[0].bit_length()):
        middle = jnp.minimum((low + high) // 2, owner.shape[0] - 1)
        below = (owner[middle] < value) & (low < high)
        low, high = jnp.where(below, middle + 1, low), jnp.where(below, high, jnp.minimum(high, middle))
    return low


def halves_body(mine, me, gate, cot, x, x_out, cot_out, gates, sems):
    slots, _, half = gates.shape
    core = me % 2 if mine else 1 - me % 2
    lanes = pl.ds(pl.multiple_of(core * half, half), half)
    copies = []
    for which, (source, target) in enumerate(((gate, gates), (cot, cot_out), (x, x_out))):
        copies.append(
            [pltpu.make_async_copy(source.at[s, :, lanes], target.at[s], sems.at[which * slots + s]) for s in range(slots)]
        )
    for s in range(slots):
        copies[0][s].start()
        copies[1][s].start()
    for s in range(slots):
        copies[2][s].start()
    return copies


def product_body(copies, gates, cot_out, w_out):
    for s in range(gates.shape[0]):
        copies[0][s].wait()
        copies[1][s].wait()
        w_out[s] = (gates[s].astype(F32) * cot_out[s].astype(F32)).astype(BF)
    for copy in copies[2]:
        copy.wait()


def lead_body(me, owner, gate, cot, x, send, meta, gates, cots, sems):
    copies = halves_body(False, me[0], gate, cot, x, send.at[0], cots, gates, sems)
    core = me[0] % 2
    base = me[0] - core
    for i in range(3):
        meta[i] = lower_bound(owner, base + i)
    meta[3] = core
    for i in range(4, 8):
        meta[i] = 0
    product_body(copies, gates, cots, send.at[1])


def lead(me, owner, gate, cot, x):
    slots, rows, width = x.shape
    half = width // 2
    return pl.pallas_call(
        lead_body,
        in_specs=[SMEM, SMEM, HBM, HBM, HBM],
        out_specs=[VMEM, SMEM],
        scratch_shapes=[pltpu.VMEM((slots, rows, half), BF)] * 2 + [pltpu.SemaphoreType.DMA((3 * slots,))],
        out_shape=[
            jax.ShapeDtypeStruct((2, slots, rows, half), BF),
            jax.ShapeDtypeStruct((8,), jnp.int32),
        ],
        compiler_params=params(LEAD_LIMIT),
        cost_estimate=pl.CostEstimate(flops=1 << 20, bytes_accessed=6 << 20, transcendentals=0),
        name="lead",
    )(me, owner, gate, cot, x)


READS = 16


def rest_body(meta, support, gate, cot, x, x_out, w_out, cot_out, cot_send, reach, gates, sems):
    copies = halves_body(True, meta[3], gate, cot, x, x_out, cot_out, gates, sems)
    slots, _, half = gates.shape
    other = pl.ds(pl.multiple_of((1 - meta[3]) * half, half), half)
    extra = [
        pltpu.make_async_copy(cot.at[s, :, other], cot_send.at[s], sems.at[3 * slots + s]) for s in range(slots)
    ]
    for copy in extra:
        copy.start()
    lags, total = support.shape
    first = meta[0]
    cap = 2 * gates.shape[0]
    for s in range(-NEAR, cap):
        tile = first + s
        found = jnp.int32(0)
        for lag in range(lags):
            at = jnp.clip(tile + lag, 0, total - 1)
            found += ((tile >= 0) & (tile + lag < total) & (support[lag, at] >= 0)).astype(jnp.int32)
        reach[s + NEAR] = found
    for i in range(cap):
        at = jnp.clip(first + i, 0, total - 1)
        found = jnp.int32(0)
        for lag in range(lags):
            found += (support[lag, at] >= 0).astype(jnp.int32)
        reach[READS + i] = found
    for i in range(NEAR + cap, READS):
        reach[i] = 0
    for i in range(READS + cap, 2 * READS):
        reach[i] = 0
    product_body(copies, gates, cot_out, w_out)
    for copy in extra:
        copy.wait()


def rest(meta, support, gate, cot, x):
    slots, rows, width = x.shape
    half = width // 2
    return pl.pallas_call(
        rest_body,
        in_specs=[SMEM, SMEM, HBM, HBM, HBM],
        out_specs=[VMEM, VMEM, VMEM, VMEM, SMEM],
        scratch_shapes=[pltpu.VMEM((slots, rows, half), BF), pltpu.SemaphoreType.DMA((4 * slots,))],
        out_shape=[jax.ShapeDtypeStruct((slots, rows, half), BF)] * 4
        + [jax.ShapeDtypeStruct((2 * READS,), jnp.int32)],
        compiler_params=params(REST_LIMIT),
        cost_estimate=pl.CostEstimate(flops=1 << 20, bytes_accessed=6 << 20, transcendentals=0),
        name="rest",
    )(meta, support, gate, cot, x)


def pack_body(x_tiles, w_tiles, x_at, w_at, halos, meta, x, w, theirs, *rest):
    x_halos, w_halos = rest[:halos], rest[halos : 2 * halos]
    x_out, w_out, sems = rest[2 * halos :]
    _, _, count, _ = chip_meta(meta)
    for which, (own, out) in enumerate(((x, x_out), (w, w_out))):
        for j in range((x_tiles, w_tiles)[which]):
            sem = sems.at[which * x_tiles + j]
            index = (x_at if which == 0 else w_at)(j, count)
            mine, slot = place(meta, index)
            depth = -1 - index if which == 0 else index - count
            here = depth < 0

            @pl.when(here & mine)
            def _():
                pltpu.make_async_copy(own.at[slot], out.at[j], sem).start()

            @pl.when(here & jnp.logical_not(mine))
            def _():
                pltpu.make_async_copy(theirs.at[which, slot], out.at[j], sem).start()

            for h in range(halos):
                halo = (x_halos if which == 0 else w_halos)[h]
                inside = jnp.clip(depth - h * NEAR, 0, NEAR - 1)
                row = NEAR - 1 - inside if which == 0 else inside

                @pl.when((depth >= h * NEAR) & (depth < (h + 1) * NEAR))
                def _():
                    pltpu.make_async_copy(halo.at[row], out.at[j], sem).start()

    for which, out in enumerate((x_out, w_out)):
        for j in range((x_tiles, w_tiles)[which]):
            pltpu.make_async_copy(theirs.at[which, 0], out.at[j], sems.at[which * x_tiles + j]).wait()


def pack(meta, x, w, theirs, x_tiles, w_tiles, x_at, w_at, x_halos=(), w_halos=()):
    _, rows, half = x.shape
    halos = len(x_halos)
    loose = pl.BlockSpec(memory_space=pl.ANY)
    return pl.pallas_call(
        functools.partial(pack_body, x_tiles, w_tiles, x_at, w_at, halos),
        in_specs=[SMEM] + [loose] * (3 + 2 * halos),
        out_specs=[loose, loose],
        scratch_shapes=[pltpu.SemaphoreType.DMA((x_tiles + w_tiles,))],
        out_shape=[jax.ShapeDtypeStruct((tiles, rows, half), BF) for tiles in (x_tiles, w_tiles)],
        compiler_params=params(),
        cost_estimate=pl.CostEstimate(flops=0, bytes_accessed=x_tiles << 20, transcendentals=0),
        name="pack",
    )(meta, x, w, theirs, *x_halos, *w_halos)


def kept(live, tile):
    return jnp.where(live, tile, jnp.zeros_like(tile))


def dot(a, b):
    return jnp.dot(a, b, preferred_element_type=F32)


def reversal(rows):
    r = lax.broadcasted_iota(jnp.int32, (rows, rows), 0)
    c = lax.broadcasted_iota(jnp.int32, (rows, rows), 1)
    return jnp.where(r + c == rows - 1, 1.0, 0.0).astype(BF)


def diagonal_sums(square):
    rows, width = square.shape
    padded = jnp.concatenate([square, jnp.zeros((rows, rows), F32)], axis=1)
    skewed = pltpu.roll(padded, 0, 1, stride=1, stride_axis=0)
    total = jnp.sum(skewed, axis=0, keepdims=True)
    total = pltpu.roll(jnp.broadcast_to(total, (8, width + rows)), width + 1, 1)
    return total[:1, :width]


def lanes_of(group):
    return pl.ds(pl.multiple_of(group * GROUP, GROUP), GROUP)


def pick(mine, theirs, meta, index, group):
    own, slot = place(meta, index)
    return jnp.where(own, mine[slot, :, lanes_of(group)], theirs[slot, :, lanes_of(group)])


def band(row, shift):
    rows, width = GROUP, row.shape[1]
    spread = jnp.broadcast_to(jnp.concatenate([row, jnp.zeros((1, rows), F32)], axis=1), (rows, width + rows))
    return pltpu.roll(spread, shift, 1, stride=1, stride_axis=0)[:, :width].astype(BF)


def own_body(lags, base, steps, groups, meta, reach, filt, x, theirs, w,
             conv_out, adj_out, fwd_out, bwd_out, sums_out, flip, xs, xl, ws, turned):
    cap, rows, _ = xs.shape
    _, _, count, _ = chip_meta(meta)
    width = filt.shape[1]
    ahead = [jnp.minimum(reach[s + NEAR], count - s) for s in range(cap)]
    behind = [reach[READS + i] for i in range(cap)]
    mine = filt[pl.ds(pl.multiple_of(meta[3] * groups, groups), groups), :].astype(BF)
    for k in range(lags):
        block = mine[:, (lags - 1 - k) * rows : (lags - k) * rows]
        flip[:, k * rows : (k + 1) * rows] = dot(block, reversal(rows))

    def one(step, carry):
        group = base + step
        row = pl.ds(meta[3] * groups + group, 1)
        bwd_out[step] = band(filt[row, :].astype(BF).astype(F32), 0)
        fwd_out[step] = band(flip[pl.ds(group, 1), :], width + 1)
        for s in range(cap):
            tile = pick(x, theirs.at[0], meta, s, group)
            xs[s] = tile
            xl[:, s * rows : (s + 1) * rows] = tile
            tile = pick(w, theirs.at[1], meta, s, group)
            ws[s] = tile
            turned[s] = tile.T
        lanes = lanes_of(step)
        for i in range(cap):
            right = jnp.concatenate([kept(i - s < behind[i], xs[s]) for s in range(i + 1)], axis=0)
            conv_out[i, :, lanes] = dot(fwd_out[step, :, (lags - 1 - i) * rows :], right)
        for s in range(cap):
            right = jnp.concatenate([kept(k < ahead[s], ws[s + k]) for k in range(cap - s)], axis=0)
            adj_out[s, :, lanes] = dot(bwd_out[step, :, : (cap - s) * rows], right)
        back = dot(reversal(rows), xl[...]).astype(BF)
        squares = []
        for k in range(0, lags, 2):
            right = [
                [kept(q < ahead[s], turned[s + q]) if s + q < cap else jnp.zeros((GROUP, rows), BF) for q in (k, k + 1)]
                for s in range(cap - k)
            ]
            right = jnp.concatenate([jnp.concatenate(pair, axis=1) for pair in right], axis=0)
            squares.append(dot(back[:, : (cap - k) * rows], right))
        sums_out[pl.ds(step, 1), :] = diagonal_sums(jnp.concatenate(squares, axis=1))
        return carry

    lax.fori_loop(0, steps, one, 0)


def own_pairs(meta, reach, filt, x, w, theirs, lags, base, steps):
    slots, rows, half = x.shape
    groups = half // GROUP
    taps = filt.shape[1]
    cap = 2 * slots
    return pl.pallas_call(
        functools.partial(own_body, lags, base, steps, groups),
        in_specs=[SMEM, SMEM] + [VMEM] * 4,
        out_specs=[VMEM] * 5,
        scratch_shapes=[
            pltpu.VMEM((groups, taps), F32),
            pltpu.VMEM((cap, rows, GROUP), BF),
            pltpu.VMEM((rows, cap * GROUP), BF),
            pltpu.VMEM((cap, rows, GROUP), BF),
            pltpu.VMEM((cap, GROUP, rows), BF),
        ],
        out_shape=[
            jax.ShapeDtypeStruct((cap, rows, steps * GROUP), F32),
            jax.ShapeDtypeStruct((cap, rows, steps * GROUP), F32),
            jax.ShapeDtypeStruct((steps, rows, taps), BF),
            jax.ShapeDtypeStruct((steps, rows, taps), BF),
            jax.ShapeDtypeStruct((steps, taps), F32),
        ],
        compiler_params=params(),
        cost_estimate=pl.CostEstimate(flops=steps * 1_000_000_000, bytes_accessed=steps << 20, transcendentals=0),
        name="own_pairs",
    )(meta, reach, filt, x, theirs, w)


def cross_body(lags, norm, meta, reach, prior, more, x, theirs, w, xn, wn,
               sums_out, xl, near, deep):
    rows = xl.shape[0]
    blocks = lags - 1
    _, _, count, _ = chip_meta(meta)
    split = blocks - NEAR
    found = []
    for p in range(blocks):
        s = p - blocks if p >= split else count - 1 - (blocks - 1 - p)
        number = reach[s + NEAR]
        found.append(number if p >= split else jnp.where(s >= 0, number, 0))
    steps = prior.shape[0]
    for part in range(2):
        source = (prior, more)[part]

        def one(step, carry):
            group = part * steps + step
            lanes = lanes_of(group)
            for p in range(split):
                index = count - 1 - (blocks - 1 - p)
                xl[:, p * rows : (p + 1) * rows] = pick(x, theirs.at[0], meta, index, group)
            for p in range(NEAR):
                at = split + p
                xl[:, at * rows : (at + 1) * rows] = xn[p, :, lanes]
            for t in range(blocks):
                tile = pick(w, theirs.at[1], meta, t, group)
                if t >= NEAR:
                    tile = jnp.where(t < count, tile, wn[jnp.clip(t - count, 0, ABOVE - 1), :, lanes])
                near[t] = tile.T
            for a in range(split):
                deep[a] = wn[a, :, lanes].T
            back = dot(reversal(rows), xl[...]).astype(BF)

            def tile_at(p, k):
                s = p - blocks
                if p >= split and s + k >= 0:
                    return kept(k < found[p], near[s + k])
                if p < split and s + k >= 0:
                    return kept(k < found[p], deep[s + k])
                return jnp.zeros((GROUP, rows), BF)

            squares = []
            for k in range(0, lags, 2):
                low = blocks - 1 - k
                right = [jnp.concatenate([tile_at(p, k), tile_at(p, k + 1)], axis=1) for p in range(low, blocks)]
                squares.append(dot(back[:, low * rows :], jnp.concatenate(right, axis=0)))
            total_sum = diagonal_sums(jnp.concatenate(squares, axis=1))
            sums_out[pl.ds(group, 1), :] = (source[pl.ds(step, 1), :] + total_sum) * norm
            return carry

        lax.fori_loop(0, steps, one, 0, unroll=2)


def cross_squares(meta, reach, prior, more, x, w, theirs, x_halo, w_halo, lags, norm):
    slots, rows, half = x.shape
    groups = half // GROUP
    taps = prior.shape[1]
    blocks = lags - 1
    return pl.pallas_call(
        functools.partial(cross_body, lags, norm),
        in_specs=[SMEM, SMEM] + [VMEM] * 7,
        out_specs=VMEM,
        scratch_shapes=[
            pltpu.VMEM((rows, blocks * GROUP), BF),
            pltpu.VMEM((blocks, GROUP, rows), BF),
            pltpu.VMEM((blocks - NEAR, GROUP, rows), BF),
        ],
        out_shape=jax.ShapeDtypeStruct((groups, taps), F32),
        compiler_params=params(),
        cost_estimate=pl.CostEstimate(flops=3_000_000_000, bytes_accessed=6 << 20, transcendentals=0),
        name="cross_squares",
    )(meta, reach, prior, more, x, theirs, w, x_halo, w_halo)


def near_body(lags, meta, reach, conv_a, conv_b, adj_a, adj_b, fwd_a, fwd_b, bwd_a, bwd_b,
              xn, wn, cot, cot_t, gate_out, input_out, send_out, conv_out, adj_out, accum):
    slots, rows, _ = gate_out.shape
    cap = 2 * slots
    _, low, count, core = chip_meta(meta)
    high = count - low
    blocks = lags - 1
    behind = [reach[READS + i] for i in range(blocks)]
    ahead = [reach[NEAR + count - 1 - c] for c in range(blocks)]
    steps = fwd_a.shape[0]
    for part in range(2):
        conv, adj, fwd, bwd = ((conv_a, adj_a, fwd_a, bwd_a), (conv_b, adj_b, fwd_b, bwd_b))[part]

        def one(step, carry):
            group = part * steps + step
            lanes, local = lanes_of(group), lanes_of(step)
            xs = [xn[p, :, lanes] for p in range(NEAR)]
            ws = [wn[p, :, lanes] for p in range(ABOVE)]
            for i in range(blocks):
                farthest = min(blocks, i + NEAR)
                start = (blocks - farthest) * rows
                size = (farthest - i) * rows
                right = [kept(lag < behind[i], xs[i + NEAR - lag]) for lag in range(farthest, i, -1)]
                term = dot(fwd[step, :, start : start + size], jnp.concatenate(right, axis=0))
                accum[i] = conv[i, :, local] + term
            accum[blocks] = conv[blocks, :, local]
            for i in range(blocks - NEAR):
                conv_out[i, :, lanes] = accum[i]
            for c in range(blocks):
                tiles = min(ABOVE, blocks - c)
                start = (c + 1) * rows
                right = jnp.concatenate([kept(c + 1 + a < ahead[c], ws[a]) for a in range(tiles)], axis=0)
                term = dot(bwd[step, :, start : start + tiles * rows], right)
                accum[cap + blocks + count - 1 - c] = term
            for c in range(blocks, cap):
                accum[cap + blocks + count - 1 - c] = jnp.zeros((rows, GROUP), F32)
            for c in range(blocks - ABOVE):
                at = count - 1 - c
                adj_out[c, :, lanes] = adj[at, :, local] + accum[cap + blocks + at]
            for slot in range(slots):
                for own in (True, False):
                    second = core if own else 1 - core
                    index = jnp.minimum(slot + second * low, cap - 1)
                    live = slot < jnp.where(second == 1, high, low)
                    cot_tile = (cot if own else cot_t)[slot, :, lanes]
                    grad = jnp.where(live, cot_tile.astype(F32) * accum[index], 0.0).astype(BF)
                    sum_ = adj[index, :, local] + accum[cap + blocks + index]
                    back = jnp.where(live, sum_, 0.0).astype(BF)
                    if own:
                        gate_out[slot, :, lanes] = grad
                        input_out[slot, :, lanes] = back
                    else:
                        send_out[0, slot, :, lanes] = grad
                        send_out[1, slot, :, lanes] = back
            return carry

        lax.fori_loop(0, steps, one, 0)


def near_pairs(meta, reach, one, two, x_halo, w_halo, cot, cot_theirs, lags):
    slots, rows, half = cot.shape
    far = lags - 1 - NEAR
    pieces = [value for pair in zip(one, two) for value in pair]
    return pl.pallas_call(
        functools.partial(near_body, lags),
        in_specs=[SMEM, SMEM] + [VMEM] * 12,
        out_specs=[VMEM] * 5,
        scratch_shapes=[
            pltpu.VMEM((4 * slots + lags - 1, rows, GROUP), F32),
        ],
        out_shape=[
            jax.ShapeDtypeStruct((slots, rows, half), BF),
            jax.ShapeDtypeStruct((slots, rows, half), BF),
            jax.ShapeDtypeStruct((2, slots, rows, half), BF),
            jax.ShapeDtypeStruct((far, rows, half), F32),
            jax.ShapeDtypeStruct((lags - 1 - ABOVE, rows, half), F32),
        ],
        compiler_params=params(),
        cost_estimate=pl.CostEstimate(flops=3_000_000_000, bytes_accessed=8 << 20, transcendentals=0),
        name="near_pairs",
    )(meta, reach, *pieces, x_halo, w_halo, cot, cot_theirs)


def far_body(lags, meta, reach, conv, adj, fwd_a, fwd_b, bwd_a, bwd_b, xf, wf, cot, cot_t,
             gate_in, input_in, send_in, gate_out, input_out, send_out):
    far, rows, _ = xf.shape
    high = wf.shape[0]
    _, _, count, _ = chip_meta(meta)
    behind = [reach[READS + i] for i in range(far)]
    ahead = [reach[NEAR + count - 1 - c] for c in range(high)]
    steps = fwd_a.shape[0]
    for part in range(2):
        fwd, bwd = ((fwd_a, bwd_a), (fwd_b, bwd_b))[part]

        def one(step, carry):
            group = part * steps + step
            lanes = lanes_of(group)
            xs = [xf[p, :, lanes] for p in range(far)]
            ws = [wf[p, :, lanes] for p in range(high)]
            results = []
            for i in range(far):
                right = [kept(lags - 1 + i - p < behind[i], xs[p]) for p in range(i, far)]
                term = dot(fwd[step, :, : (far - i) * rows], jnp.concatenate(right, axis=0))
                value = pick(cot, cot_t, meta, i, group).astype(F32) * (conv[i, :, lanes] + term)
                results.append((i, gate_out, 0, value.astype(BF)))
            for c in range(high):
                right = [kept(c + ABOVE + 1 + a < ahead[c], ws[a]) for a in range(high - c)]
                term = dot(bwd[step, :, (c + ABOVE + 1) * rows :], jnp.concatenate(right, axis=0))
                results.append((count - 1 - c, input_out, 1, (adj[c, :, lanes] + term).astype(BF)))
            for index, out, which, value in results:
                mine, slot = place(meta, index)

                @pl.when(mine)
                def _():
                    out[slot, :, lanes] = value

                @pl.when(jnp.logical_not(mine))
                def _():
                    send_out[which, slot, :, lanes] = value

            return carry

        lax.fori_loop(0, steps, one, 0)


def far_pairs(meta, reach, conv, adj, one, two, x_halo, w_halo, cot, cot_theirs, gate, inp, send, lags):
    pieces = [one[2], two[2], one[3], two[3]]
    return pl.pallas_call(
        functools.partial(far_body, lags),
        in_specs=[SMEM, SMEM] + [VMEM] * 13,
        out_specs=[VMEM] * 3,
        out_shape=[
            jax.ShapeDtypeStruct(gate.shape, BF),
            jax.ShapeDtypeStruct(inp.shape, BF),
            jax.ShapeDtypeStruct(send.shape, BF),
        ],
        input_output_aliases={12: 0, 13: 1, 14: 2},
        compiler_params=params(),
        cost_estimate=pl.CostEstimate(flops=800_000_000, bytes_accessed=4 << 20, transcendentals=0),
        name="far_pairs",
    )(meta, reach, conv, adj, *pieces, x_halo, w_halo, cot, cot_theirs, gate, inp, send)


def settle_body(mine, meta, gate, inp, gate_in, input_in, gate_out, input_out, sems):
    slots, _, half = gate.shape
    core = meta[3] if mine else 1 - meta[3]
    lanes = pl.ds(pl.multiple_of(core * half, half), half)
    copies = []
    for which, (source, out) in enumerate(((gate, gate_out), (inp, input_out))):
        for s in range(slots):
            copies.append(pltpu.make_async_copy(source.at[s], out.at[s, :, lanes], sems.at[which * slots + s]))
    for copy in copies:
        copy.start()
    for copy in copies:
        copy.wait()


def place_mine(meta, gate, inp):
    slots, rows, half = gate.shape

    def body(meta, gate, inp, gate_out, input_out, sems):
        settle_body(True, meta, gate, inp, None, None, gate_out, input_out, sems)

    loose = pl.BlockSpec(memory_space=pl.ANY)
    return pl.pallas_call(
        body,
        in_specs=[SMEM, VMEM, VMEM],
        out_specs=[loose, loose],
        scratch_shapes=[pltpu.SemaphoreType.DMA((2 * slots,))],
        out_shape=[jax.ShapeDtypeStruct((slots, rows, 2 * half), BF)] * 2,
        compiler_params=params(),
        name="place_mine",
    )(meta, gate, inp)


def join(meta, got, gate, inp, sums, moved):
    slots = gate.shape[0]
    groups, taps = sums.shape

    def body(meta, got, gate_in, input_in, sums, pair, other, other_pair, gate_out, input_out, filter_out, sems):
        core = meta[3]
        filter_out[pl.ds(pl.multiple_of(core * groups, groups), groups), :] = sums[...] + pair[...]
        filter_out[pl.ds(pl.multiple_of((1 - core) * groups, groups), groups), :] = other[...] + other_pair[...]
        settle_body(False, meta, got.at[0], got.at[1], gate_in, input_in, gate_out, input_out, sems)

    loose = pl.BlockSpec(memory_space=pl.ANY)
    return pl.pallas_call(
        body,
        in_specs=[SMEM, VMEM, loose, loose, VMEM, VMEM, VMEM, VMEM],
        out_specs=[loose, loose, VMEM],
        scratch_shapes=[pltpu.SemaphoreType.DMA((2 * slots,))],
        out_shape=[
            jax.ShapeDtypeStruct(gate.shape, BF),
            jax.ShapeDtypeStruct(inp.shape, BF),
            jax.ShapeDtypeStruct((2 * groups, taps), F32),
        ],
        input_output_aliases={2: 0, 3: 1},
        compiler_params=params(),
        name="join",
    )(meta, got, gate, inp, sums, *moved)


def per_device(conv_input, gate_signal, cotangent, filters, tile_owner, support):
    slots, rows, width = conv_input.shape
    lags = support.shape[1]
    filter_count, taps = filters.shape
    total = tile_owner.shape[0]
    tie = lax.optimization_barrier
    me = lax.axis_index("ctx")
    core = me % 2

    def up(value):
        return shifted(value, "ctx", 2)

    def down(value):
        return shifted(value, "ctx", -2)

    norm = 1.0 / math.sqrt(total * rows * width * lax.axis_size("ch") / filter_count)
    send, meta = lead(me.reshape(1), tile_owner, gate_signal, cotangent, conv_input)
    theirs = swapped(send, "ctx", 1)
    x, w, cot, cot_send, reach = rest(meta, support.T, gate_signal, cotangent, conv_input)
    xs, ws = pack(meta, x, w, theirs, NEAR, ABOVE, lambda j, n: n - NEAR + j, lambda j, n: j)
    x0, w0 = up(xs), down(ws)
    cot_theirs = swapped(cot_send, "ctx", 1)
    half_groups = width // 2 // GROUP // 2
    one = own_pairs(meta, reach, filters, x, w, theirs, lags, 0, half_groups)
    two = own_pairs(meta, reach, filters, x, w, theirs, lags, half_groups, half_groups)
    x0, w0, one, two = tie((x0, w0, one, two))
    *one, first_sums = one
    *two, second_sums = two
    xs, ws = pack(
        meta, x, w, theirs, lags - 1 - NEAR, lags - 1 - ABOVE,
        lambda j, n: n - lags + 1 + j, lambda j, n: ABOVE + j, (x0,), (w0,)
    )
    xs, ws, first_sums, second_sums = tie((xs, ws, first_sums, second_sums))
    w2, x2 = down(ws), up(xs)
    sums = cross_squares(meta, reach, first_sums, second_sums, x, w, theirs, x0, w0, lags, norm)

    def stage(sums, axis, masks, filler):
        moved = [swapped(sums, axis, mask) for mask in masks]
        out = filler(tie((sums, meta))[1])
        total_sum = sums + moved[0]
        if len(masks) == 3:
            total_sum = total_sum + (moved[1] + moved[2])
        return tie((total_sum, out))

    def close(meta):
        return near_pairs(meta, reach, one, two, x0, w0, cot, cot_theirs, lags)

    sums, (gate, inp, back, conv, adj) = stage(sums, "ch", (1, 2, 3), close)

    def finish(meta):
        return far_pairs(
            meta, reach, conv, adj, one, two, x2, w2, cot, cot_theirs, gate, inp, back, lags
        )

    sums, (gate, inp, back) = stage(sums, "ctx", (8, 16, 24), finish)
    got = swapped(back, "ctx", 1)
    sums, (gate, inp) = stage(sums, "ctx", (2, 4, 6), lambda meta: place_mine(meta, gate, inp))
    count = lax.axis_size("ctx")
    low = count // 8 - 1
    mirrored = [(a, a ^ (count - 1 - low)) for a in range(count)]
    moved = [
        lax.ppermute(sums, "ctx", mirrored),
        swapped(sums, "ctx", 1),
        lax.ppermute(sums, "ctx", [(a, b ^ 1) for a, b in mirrored]),
    ]
    return join(meta, got, gate, inp, sums, moved)


def solution(mesh):
    return jax.shard_map(
        per_device,
        mesh=mesh,
        in_specs=(P("ctx", None, "ch"), P("ctx", None, "ch"), P("ctx", None, "ch"), P(), P(), P()),
        out_specs=(P("ctx", None, "ch"), P("ctx", None, "ch"), P()),
        check_vma=False,
    )
```

```python
import functools
import math

import jax
import jax.numpy as jnp
from jax import lax
from jax.experimental import pallas as pl
from jax.experimental.pallas import tpu as pltpu
from jax.sharding import PartitionSpec as P

GROUP = 128
NEAR = 4
ABOVE = 3
BF = jnp.bfloat16
F32 = jnp.float32
VMEM_LIMIT = 8 * 1024 * 1024
LEAD_LIMIT = 56 * 1024 * 1024
REST_LIMIT = 50 * 1024 * 1024


def params(limit=VMEM_LIMIT):
    return pltpu.CompilerParams(vmem_limit_bytes=limit)


def shifted(value, axis, steps):
    count = lax.axis_size(axis)
    pairs = [(a, a + steps) for a in range(max(0, -steps), min(count, count - steps))]
    return lax.ppermute(value, axis, pairs)


def swapped(value, axis, mask):
    count = lax.axis_size(axis)
    return lax.ppermute(value, axis, [(a, a ^ mask) for a in range(count)])


def chip_meta(meta):
    first, second, end, core = meta[0], meta[1], meta[2], meta[3]
    return first, second - first, end - first, core


def place(meta, index):
    _, low, _, core = chip_meta(meta)
    on_second = (index >= low).astype(jnp.int32)
    slot = jnp.clip(index - on_second * low, 0, 3)
    return on_second == core, slot


SMEM = pl.BlockSpec(memory_space=pltpu.SMEM)
VMEM = pl.BlockSpec(memory_space=pltpu.VMEM)


HBM = pl.BlockSpec(memory_space=pltpu.HBM)


def lower_bound(owner, value):
    low, high = jnp.int32(0), jnp.int32(owner.shape[0])
    for _ in range(owner.shape[0].bit_length()):
        middle = jnp.minimum((low + high) // 2, owner.shape[0] - 1)
        below = (owner[middle] < value) & (low < high)
        low, high = jnp.where(below, middle + 1, low), jnp.where(below, high, jnp.minimum(high, middle))
    return low


def halves_body(mine, me, gate, cot, x, x_out, cot_out, gates, sems):
    slots, _, half = gates.shape
    core = me % 2 if mine else 1 - me % 2
    lanes = pl.ds(pl.multiple_of(core * half, half), half)
    copies = []
    for which, (source, target) in enumerate(((gate, gates), (cot, cot_out), (x, x_out))):
        copies.append(
            [pltpu.make_async_copy(source.at[s, :, lanes], target.at[s], sems.at[which * slots + s]) for s in range(slots)]
        )
    for s in range(slots):
        copies[0][s].start()
        copies[1][s].start()
    for s in range(slots):
        copies[2][s].start()
    return copies


def product_body(copies, gates, cot_out, w_out):
    for s in range(gates.shape[0]):
        copies[0][s].wait()
        copies[1][s].wait()
        w_out[s] = (gates[s].astype(F32) * cot_out[s].astype(F32)).astype(BF)
    for copy in copies[2]:
        copy.wait()


def lead_body(me, owner, gate, cot, x, send, meta, gates, cots, sems):
    copies = halves_body(False, me[0], gate, cot, x, send.at[0], cots, gates, sems)
    core = me[0] % 2
    base = me[0] - core
    for i in range(3):
        meta[i] = lower_bound(owner, base + i)
    meta[3] = core
    for i in range(4, 8):
        meta[i] = 0
    product_body(copies, gates, cots, send.at[1])


def lead(me, owner, gate, cot, x):
    slots, rows, width = x.shape
    half = width // 2
    return pl.pallas_call(
        lead_body,
        in_specs=[SMEM, SMEM, HBM, HBM, HBM],
        out_specs=[VMEM, SMEM],
        scratch_shapes=[pltpu.VMEM((slots, rows, half), BF)] * 2 + [pltpu.SemaphoreType.DMA((3 * slots,))],
        out_shape=[
            jax.ShapeDtypeStruct((2, slots, rows, half), BF),
            jax.ShapeDtypeStruct((8,), jnp.int32),
        ],
        compiler_params=params(LEAD_LIMIT),
        cost_estimate=pl.CostEstimate(flops=1 << 20, bytes_accessed=6 << 20, transcendentals=0),
        name="lead",
    )(me, owner, gate, cot, x)


READS = 16


def rest_body(meta, support, gate, cot, x, x_out, w_out, cot_out, cot_send, reach, gates, sems):
    copies = halves_body(True, meta[3], gate, cot, x, x_out, cot_out, gates, sems)
    slots, _, half = gates.shape
    other = pl.ds(pl.multiple_of((1 - meta[3]) * half, half), half)
    extra = [
        pltpu.make_async_copy(cot.at[s, :, other], cot_send.at[s], sems.at[3 * slots + s]) for s in range(slots)
    ]
    for copy in extra:
        copy.start()
    lags, total = support.shape
    first = meta[0]
    cap = 2 * gates.shape[0]
    for s in range(-NEAR, cap):
        tile = first + s
        found = jnp.int32(0)
        for lag in range(lags):
            at = jnp.clip(tile + lag, 0, total - 1)
            found += ((tile >= 0) & (tile + lag < total) & (support[lag, at] >= 0)).astype(jnp.int32)
        reach[s + NEAR] = found
    for i in range(cap):
        at = jnp.clip(first + i, 0, total - 1)
        found = jnp.int32(0)
        for lag in range(lags):
            found += (support[lag, at] >= 0).astype(jnp.int32)
        reach[READS + i] = found
    for i in range(NEAR + cap, READS):
        reach[i] = 0
    for i in range(READS + cap, 2 * READS):
        reach[i] = 0
    product_body(copies, gates, cot_out, w_out)
    for copy in extra:
        copy.wait()


def rest(meta, support, gate, cot, x):
    slots, rows, width = x.shape
    half = width // 2
    return pl.pallas_call(
        rest_body,
        in_specs=[SMEM, SMEM, HBM, HBM, HBM],
        out_specs=[VMEM, VMEM, VMEM, VMEM, SMEM],
        scratch_shapes=[pltpu.VMEM((slots, rows, half), BF), pltpu.SemaphoreType.DMA((4 * slots,))],
        out_shape=[jax.ShapeDtypeStruct((slots, rows, half), BF)] * 4
        + [jax.ShapeDtypeStruct((2 * READS,), jnp.int32)],
        compiler_params=params(REST_LIMIT),
        cost_estimate=pl.CostEstimate(flops=1 << 20, bytes_accessed=6 << 20, transcendentals=0),
        name="rest",
    )(meta, support, gate, cot, x)


def pack_body(x_tiles, w_tiles, x_at, w_at, halos, meta, x, w, theirs, *rest):
    x_halos, w_halos = rest[:halos], rest[halos : 2 * halos]
    x_out, w_out, sems = rest[2 * halos :]
    _, _, count, _ = chip_meta(meta)
    for which, (own, out) in enumerate(((x, x_out), (w, w_out))):
        for j in range((x_tiles, w_tiles)[which]):
            sem = sems.at[which * x_tiles + j]
            index = (x_at if which == 0 else w_at)(j, count)
            mine, slot = place(meta, index)
            depth = -1 - index if which == 0 else index - count
            here = depth < 0

            @pl.when(here & mine)
            def _():
                pltpu.make_async_copy(own.at[slot], out.at[j], sem).start()

            @pl.when(here & jnp.logical_not(mine))
            def _():
                pltpu.make_async_copy(theirs.at[which, slot], out.at[j], sem).start()

            for h in range(halos):
                halo = (x_halos if which == 0 else w_halos)[h]
                inside = jnp.clip(depth - h * NEAR, 0, NEAR - 1)
                row = NEAR - 1 - inside if which == 0 else inside

                @pl.when((depth >= h * NEAR) & (depth < (h + 1) * NEAR))
                def _():
                    pltpu.make_async_copy(halo.at[row], out.at[j], sem).start()

    for which, out in enumerate((x_out, w_out)):
        for j in range((x_tiles, w_tiles)[which]):
            pltpu.make_async_copy(theirs.at[which, 0], out.at[j], sems.at[which * x_tiles + j]).wait()


def pack(meta, x, w, theirs, x_tiles, w_tiles, x_at, w_at, x_halos=(), w_halos=()):
    _, rows, half = x.shape
    halos = len(x_halos)
    loose = pl.BlockSpec(memory_space=pl.ANY)
    return pl.pallas_call(
        functools.partial(pack_body, x_tiles, w_tiles, x_at, w_at, halos),
        in_specs=[SMEM] + [loose] * (3 + 2 * halos),
        out_specs=[loose, loose],
        scratch_shapes=[pltpu.SemaphoreType.DMA((x_tiles + w_tiles,))],
        out_shape=[jax.ShapeDtypeStruct((tiles, rows, half), BF) for tiles in (x_tiles, w_tiles)],
        compiler_params=params(),
        cost_estimate=pl.CostEstimate(flops=0, bytes_accessed=x_tiles << 20, transcendentals=0),
        name="pack",
    )(meta, x, w, theirs, *x_halos, *w_halos)


def kept(live, tile):
    return jnp.where(live, tile, jnp.zeros_like(tile))


def dot(a, b):
    return jnp.dot(a, b, preferred_element_type=F32)


def reversal(rows):
    r = lax.broadcasted_iota(jnp.int32, (rows, rows), 0)
    c = lax.broadcasted_iota(jnp.int32, (rows, rows), 1)
    return jnp.where(r + c == rows - 1, 1.0, 0.0).astype(BF)


def diagonal_sums(square):
    rows, width = square.shape
    padded = jnp.concatenate([square, jnp.zeros((rows, rows), F32)], axis=1)
    skewed = pltpu.roll(padded, 0, 1, stride=1, stride_axis=0)
    total = jnp.sum(skewed, axis=0, keepdims=True)
    total = pltpu.roll(jnp.broadcast_to(total, (8, width + rows)), width + 1, 1)
    return total[:1, :width]


def lanes_of(group):
    return pl.ds(pl.multiple_of(group * GROUP, GROUP), GROUP)


def pick(mine, theirs, meta, index, group):
    own, slot = place(meta, index)
    return jnp.where(own, mine[slot, :, lanes_of(group)], theirs[slot, :, lanes_of(group)])


def band(row, shift):
    rows, width = GROUP, row.shape[1]
    spread = jnp.broadcast_to(jnp.concatenate([row, jnp.zeros((1, rows), F32)], axis=1), (rows, width + rows))
    return pltpu.roll(spread, shift, 1, stride=1, stride_axis=0)[:, :width].astype(BF)


def own_body(lags, base, steps, groups, meta, reach, filt, x, theirs, w,
             conv_out, adj_out, fwd_out, bwd_out, sums_out, flip, xs, xl, ws, turned):
    cap, rows, _ = xs.shape
    _, _, count, _ = chip_meta(meta)
    width = filt.shape[1]
    ahead = [jnp.minimum(reach[s + NEAR], count - s) for s in range(cap)]
    behind = [reach[READS + i] for i in range(cap)]
    mine = filt[pl.ds(pl.multiple_of(meta[3] * groups, groups), groups), :].astype(BF)
    for k in range(lags):
        block = mine[:, (lags - 1 - k) * rows : (lags - k) * rows]
        flip[:, k * rows : (k + 1) * rows] = dot(block, reversal(rows))

    def one(step, carry):
        group = base + step
        row = pl.ds(meta[3] * groups + group, 1)
        bwd_out[step] = band(filt[row, :].astype(BF).astype(F32), 0)
        fwd_out[step] = band(flip[pl.ds(group, 1), :], width + 1)
        for s in range(cap):
            tile = pick(x, theirs.at[0], meta, s, group)
            xs[s] = tile
            xl[:, s * rows : (s + 1) * rows] = tile
            tile = pick(w, theirs.at[1], meta, s, group)
            ws[s] = tile
            turned[s] = tile.T
        lanes = lanes_of(step)
        for i in range(cap):
            right = jnp.concatenate([kept(i - s < behind[i], xs[s]) for s in range(i + 1)], axis=0)
            conv_out[i, :, lanes] = dot(fwd_out[step, :, (lags - 1 - i) * rows :], right)
        for s in range(cap):
            right = jnp.concatenate([kept(k < ahead[s], ws[s + k]) for k in range(cap - s)], axis=0)
            adj_out[s, :, lanes] = dot(bwd_out[step, :, : (cap - s) * rows], right)
        back = dot(reversal(rows), xl[...]).astype(BF)
        squares = []
        for k in range(0, lags, 2):
            right = [
                [kept(q < ahead[s], turned[s + q]) if s + q < cap else jnp.zeros((GROUP, rows), BF) for q in (k, k + 1)]
                for s in range(cap - k)
            ]
            right = jnp.concatenate([jnp.concatenate(pair, axis=1) for pair in right], axis=0)
            squares.append(dot(back[:, : (cap - k) * rows], right))
        sums_out[pl.ds(step, 1), :] = diagonal_sums(jnp.concatenate(squares, axis=1))
        return carry

    lax.fori_loop(0, steps, one, 0)


def own_pairs(meta, reach, filt, x, w, theirs, lags, base, steps):
    slots, rows, half = x.shape
    groups = half // GROUP
    taps = filt.shape[1]
    cap = 2 * slots
    return pl.pallas_call(
        functools.partial(own_body, lags, base, steps, groups),
        in_specs=[SMEM, SMEM] + [VMEM] * 4,
        out_specs=[VMEM] * 5,
        scratch_shapes=[
            pltpu.VMEM((groups, taps), F32),
            pltpu.VMEM((cap, rows, GROUP), BF),
            pltpu.VMEM((rows, cap * GROUP), BF),
            pltpu.VMEM((cap, rows, GROUP), BF),
            pltpu.VMEM((cap, GROUP, rows), BF),
        ],
        out_shape=[
            jax.ShapeDtypeStruct((cap, rows, steps * GROUP), F32),
            jax.ShapeDtypeStruct((cap, rows, steps * GROUP), F32),
            jax.ShapeDtypeStruct((steps, rows, taps), BF),
            jax.ShapeDtypeStruct((steps, rows, taps), BF),
            jax.ShapeDtypeStruct((steps, taps), F32),
        ],
        compiler_params=params(),
        cost_estimate=pl.CostEstimate(flops=steps * 1_000_000_000, bytes_accessed=steps << 20, transcendentals=0),
        name="own_pairs",
    )(meta, reach, filt, x, theirs, w)


def cross_body(lags, norm, meta, reach, prior, more, x, theirs, w, xn, wn,
               sums_out, xl, near, deep):
    rows = xl.shape[0]
    blocks = lags - 1
    _, _, count, _ = chip_meta(meta)
    split = blocks - NEAR
    found = []
    for p in range(blocks):
        s = p - blocks if p >= split else count - 1 - (blocks - 1 - p)
        number = reach[s + NEAR]
        found.append(number if p >= split else jnp.where(s >= 0, number, 0))
    steps = prior.shape[0]
    for part in range(2):
        source = (prior, more)[part]

        def one(step, carry):
            group = part * steps + step
            lanes = lanes_of(group)
            for p in range(split):
                index = count - 1 - (blocks - 1 - p)
                xl[:, p * rows : (p + 1) * rows] = pick(x, theirs.at[0], meta, index, group)
            for p in range(NEAR):
                at = split + p
                xl[:, at * rows : (at + 1) * rows] = xn[p, :, lanes]
            for t in range(blocks):
                tile = pick(w, theirs.at[1], meta, t, group)
                if t >= NEAR:
                    tile = jnp.where(t < count, tile, wn[jnp.clip(t - count, 0, ABOVE - 1), :, lanes])
                near[t] = tile.T
            for a in range(split):
                deep[a] = wn[a, :, lanes].T
            back = dot(reversal(rows), xl[...]).astype(BF)

            def tile_at(p, k):
                s = p - blocks
                if p >= split and s + k >= 0:
                    return kept(k < found[p], near[s + k])
                if p < split and s + k >= 0:
                    return kept(k < found[p], deep[s + k])
                return jnp.zeros((GROUP, rows), BF)

            squares = []
            for k in range(0, lags, 2):
                low = blocks - 1 - k
                right = [jnp.concatenate([tile_at(p, k), tile_at(p, k + 1)], axis=1) for p in range(low, blocks)]
                squares.append(dot(back[:, low * rows :], jnp.concatenate(right, axis=0)))
            total_sum = diagonal_sums(jnp.concatenate(squares, axis=1))
            sums_out[pl.ds(group, 1), :] = (source[pl.ds(step, 1), :] + total_sum) * norm
            return carry

        lax.fori_loop(0, steps, one, 0, unroll=4)


def cross_squares(meta, reach, prior, more, x, w, theirs, x_halo, w_halo, lags, norm):
    slots, rows, half = x.shape
    groups = half // GROUP
    taps = prior.shape[1]
    blocks = lags - 1
    return pl.pallas_call(
        functools.partial(cross_body, lags, norm),
        in_specs=[SMEM, SMEM] + [VMEM] * 7,
        out_specs=VMEM,
        scratch_shapes=[
            pltpu.VMEM((rows, blocks * GROUP), BF),
            pltpu.VMEM((blocks, GROUP, rows), BF),
            pltpu.VMEM((blocks - NEAR, GROUP, rows), BF),
        ],
        out_shape=jax.ShapeDtypeStruct((groups, taps), F32),
        compiler_params=params(),
        cost_estimate=pl.CostEstimate(flops=3_000_000_000, bytes_accessed=6 << 20, transcendentals=0),
        name="cross_squares",
    )(meta, reach, prior, more, x, theirs, w, x_halo, w_halo)


def near_body(lags, meta, reach, conv_a, conv_b, adj_a, adj_b, fwd_a, fwd_b, bwd_a, bwd_b,
              xn, wn, cot, cot_t, gate_out, input_out, send_out, conv_out, adj_out, accum):
    slots, rows, _ = gate_out.shape
    cap = 2 * slots
    _, low, count, core = chip_meta(meta)
    high = count - low
    blocks = lags - 1
    behind = [reach[READS + i] for i in range(blocks)]
    ahead = [reach[NEAR + count - 1 - c] for c in range(blocks)]
    steps = fwd_a.shape[0]
    for part in range(2):
        conv, adj, fwd, bwd = ((conv_a, adj_a, fwd_a, bwd_a), (conv_b, adj_b, fwd_b, bwd_b))[part]

        def one(step, carry):
            group = part * steps + step
            lanes, local = lanes_of(group), lanes_of(step)
            xs = [xn[p, :, lanes] for p in range(NEAR)]
            ws = [wn[p, :, lanes] for p in range(ABOVE)]
            for i in range(blocks):
                farthest = min(blocks, i + NEAR)
                start = (blocks - farthest) * rows
                size = (farthest - i) * rows
                right = [kept(lag < behind[i], xs[i + NEAR - lag]) for lag in range(farthest, i, -1)]
                term = dot(fwd[step, :, start : start + size], jnp.concatenate(right, axis=0))
                accum[i] = conv[i, :, local] + term
            accum[blocks] = conv[blocks, :, local]
            for i in range(blocks - NEAR):
                conv_out[i, :, lanes] = accum[i]
            for c in range(blocks):
                tiles = min(ABOVE, blocks - c)
                start = (c + 1) * rows
                right = jnp.concatenate([kept(c + 1 + a < ahead[c], ws[a]) for a in range(tiles)], axis=0)
                term = dot(bwd[step, :, start : start + tiles * rows], right)
                accum[cap + blocks + count - 1 - c] = term
            for c in range(blocks, cap):
                accum[cap + blocks + count - 1 - c] = jnp.zeros((rows, GROUP), F32)
            for c in range(blocks - ABOVE):
                at = count - 1 - c
                adj_out[c, :, lanes] = adj[at, :, local] + accum[cap + blocks + at]
            for slot in range(slots):
                for own in (True, False):
                    second = core if own else 1 - core
                    index = jnp.minimum(slot + second * low, cap - 1)
                    live = slot < jnp.where(second == 1, high, low)
                    cot_tile = (cot if own else cot_t)[slot, :, lanes]
                    grad = jnp.where(live, cot_tile.astype(F32) * accum[index], 0.0).astype(BF)
                    sum_ = adj[index, :, local] + accum[cap + blocks + index]
                    back = jnp.where(live, sum_, 0.0).astype(BF)
                    if own:
                        gate_out[slot, :, lanes] = grad
                        input_out[slot, :, lanes] = back
                    else:
                        send_out[0, slot, :, lanes] = grad
                        send_out[1, slot, :, lanes] = back
            return carry

        lax.fori_loop(0, steps, one, 0)


def near_pairs(meta, reach, one, two, x_halo, w_halo, cot, cot_theirs, lags):
    slots, rows, half = cot.shape
    far = lags - 1 - NEAR
    pieces = [value for pair in zip(one, two) for value in pair]
    return pl.pallas_call(
        functools.partial(near_body, lags),
        in_specs=[SMEM, SMEM] + [VMEM] * 12,
        out_specs=[VMEM] * 5,
        scratch_shapes=[
            pltpu.VMEM((4 * slots + lags - 1, rows, GROUP), F32),
        ],
        out_shape=[
            jax.ShapeDtypeStruct((slots, rows, half), BF),
            jax.ShapeDtypeStruct((slots, rows, half), BF),
            jax.ShapeDtypeStruct((2, slots, rows, half), BF),
            jax.ShapeDtypeStruct((far, rows, half), F32),
            jax.ShapeDtypeStruct((lags - 1 - ABOVE, rows, half), F32),
        ],
        compiler_params=params(),
        cost_estimate=pl.CostEstimate(flops=3_000_000_000, bytes_accessed=8 << 20, transcendentals=0),
        name="near_pairs",
    )(meta, reach, *pieces, x_halo, w_halo, cot, cot_theirs)


def far_body(lags, meta, reach, conv, adj, fwd_a, fwd_b, bwd_a, bwd_b, xf, wf, cot, cot_t,
             gate_in, input_in, send_in, gate_out, input_out, send_out):
    far, rows, _ = xf.shape
    high = wf.shape[0]
    _, _, count, _ = chip_meta(meta)
    behind = [reach[READS + i] for i in range(far)]
    ahead = [reach[NEAR + count - 1 - c] for c in range(high)]
    steps = fwd_a.shape[0]
    for part in range(2):
        fwd, bwd = ((fwd_a, bwd_a), (fwd_b, bwd_b))[part]

        def one(step, carry):
            group = part * steps + step
            lanes = lanes_of(group)
            xs = [xf[p, :, lanes] for p in range(far)]
            ws = [wf[p, :, lanes] for p in range(high)]
            results = []
            for i in range(far):
                right = [kept(lags - 1 + i - p < behind[i], xs[p]) for p in range(i, far)]
                term = dot(fwd[step, :, : (far - i) * rows], jnp.concatenate(right, axis=0))
                value = pick(cot, cot_t, meta, i, group).astype(F32) * (conv[i, :, lanes] + term)
                results.append((i, gate_out, 0, value.astype(BF)))
            for c in range(high):
                right = [kept(c + ABOVE + 1 + a < ahead[c], ws[a]) for a in range(high - c)]
                term = dot(bwd[step, :, (c + ABOVE + 1) * rows :], jnp.concatenate(right, axis=0))
                results.append((count - 1 - c, input_out, 1, (adj[c, :, lanes] + term).astype(BF)))
            for index, out, which, value in results:
                mine, slot = place(meta, index)

                @pl.when(mine)
                def _():
                    out[slot, :, lanes] = value

                @pl.when(jnp.logical_not(mine))
                def _():
                    send_out[which, slot, :, lanes] = value

            return carry

        lax.fori_loop(0, steps, one, 0)


def far_pairs(meta, reach, conv, adj, one, two, x_halo, w_halo, cot, cot_theirs, gate, inp, send, lags):
    pieces = [one[2], two[2], one[3], two[3]]
    return pl.pallas_call(
        functools.partial(far_body, lags),
        in_specs=[SMEM, SMEM] + [VMEM] * 13,
        out_specs=[VMEM] * 3,
        out_shape=[
            jax.ShapeDtypeStruct(gate.shape, BF),
            jax.ShapeDtypeStruct(inp.shape, BF),
            jax.ShapeDtypeStruct(send.shape, BF),
        ],
        input_output_aliases={12: 0, 13: 1, 14: 2},
        compiler_params=params(),
        cost_estimate=pl.CostEstimate(flops=800_000_000, bytes_accessed=4 << 20, transcendentals=0),
        name="far_pairs",
    )(meta, reach, conv, adj, *pieces, x_halo, w_halo, cot, cot_theirs, gate, inp, send)


def settle_body(mine, meta, gate, inp, gate_in, input_in, gate_out, input_out, sems):
    slots, _, half = gate.shape
    core = meta[3] if mine else 1 - meta[3]
    lanes = pl.ds(pl.multiple_of(core * half, half), half)
    copies = []
    for which, (source, out) in enumerate(((gate, gate_out), (inp, input_out))):
        for s in range(slots):
            copies.append(pltpu.make_async_copy(source.at[s], out.at[s, :, lanes], sems.at[which * slots + s]))
    for copy in copies:
        copy.start()
    for copy in copies:
        copy.wait()


def place_mine(meta, gate, inp):
    slots, rows, half = gate.shape

    def body(meta, gate, inp, gate_out, input_out, sems):
        settle_body(True, meta, gate, inp, None, None, gate_out, input_out, sems)

    loose = pl.BlockSpec(memory_space=pl.ANY)
    return pl.pallas_call(
        body,
        in_specs=[SMEM, VMEM, VMEM],
        out_specs=[loose, loose],
        scratch_shapes=[pltpu.SemaphoreType.DMA((2 * slots,))],
        out_shape=[jax.ShapeDtypeStruct((slots, rows, 2 * half), BF)] * 2,
        compiler_params=params(),
        name="place_mine",
    )(meta, gate, inp)


def join(meta, got, gate, inp, sums, moved):
    slots = gate.shape[0]
    groups, taps = sums.shape

    def body(meta, got, gate_in, input_in, sums, pair, other, other_pair, gate_out, input_out, filter_out, sems):
        core = meta[3]
        filter_out[pl.ds(pl.multiple_of(core * groups, groups), groups), :] = sums[...] + pair[...]
        filter_out[pl.ds(pl.multiple_of((1 - core) * groups, groups), groups), :] = other[...] + other_pair[...]
        settle_body(False, meta, got.at[0], got.at[1], gate_in, input_in, gate_out, input_out, sems)

    loose = pl.BlockSpec(memory_space=pl.ANY)
    return pl.pallas_call(
        body,
        in_specs=[SMEM, VMEM, loose, loose, VMEM, VMEM, VMEM, VMEM],
        out_specs=[loose, loose, VMEM],
        scratch_shapes=[pltpu.SemaphoreType.DMA((2 * slots,))],
        out_shape=[
            jax.ShapeDtypeStruct(gate.shape, BF),
            jax.ShapeDtypeStruct(inp.shape, BF),
            jax.ShapeDtypeStruct((2 * groups, taps), F32),
        ],
        input_output_aliases={2: 0, 3: 1},
        compiler_params=params(),
        name="join",
    )(meta, got, gate, inp, sums, *moved)


def per_device(conv_input, gate_signal, cotangent, filters, tile_owner, support):
    slots, rows, width = conv_input.shape
    lags = support.shape[1]
    filter_count, taps = filters.shape
    total = tile_owner.shape[0]
    tie = lax.optimization_barrier
    me = lax.axis_index("ctx")
    core = me % 2

    def up(value):
        return shifted(value, "ctx", 2)

    def down(value):
        return shifted(value, "ctx", -2)

    norm = 1.0 / math.sqrt(total * rows * width * lax.axis_size("ch") / filter_count)
    send, meta = lead(me.reshape(1), tile_owner, gate_signal, cotangent, conv_input)
    theirs = swapped(send, "ctx", 1)
    x, w, cot, cot_send, reach = rest(meta, support.T, gate_signal, cotangent, conv_input)
    xs, ws = pack(meta, x, w, theirs, NEAR, ABOVE, lambda j, n: n - NEAR + j, lambda j, n: j)
    x0, w0 = up(xs), down(ws)
    cot_theirs = swapped(cot_send, "ctx", 1)
    half_groups = width // 2 // GROUP // 2
    one = own_pairs(meta, reach, filters, x, w, theirs, lags, 0, half_groups)
    two = own_pairs(meta, reach, filters, x, w, theirs, lags, half_groups, half_groups)
    x0, w0, one, two = tie((x0, w0, one, two))
    *one, first_sums = one
    *two, second_sums = two
    xs, ws = pack(
        meta, x, w, theirs, lags - 1 - NEAR, lags - 1 - ABOVE,
        lambda j, n: n - lags + 1 + j, lambda j, n: ABOVE + j, (x0,), (w0,)
    )
    xs, ws, first_sums, second_sums = tie((xs, ws, first_sums, second_sums))
    w2, x2 = down(ws), up(xs)
    sums = cross_squares(meta, reach, first_sums, second_sums, x, w, theirs, x0, w0, lags, norm)

    def stage(sums, axis, masks, filler):
        moved = [swapped(sums, axis, mask) for mask in masks]
        out = filler(tie((sums, meta))[1])
        total_sum = sums + moved[0]
        if len(masks) == 3:
            total_sum = total_sum + (moved[1] + moved[2])
        return tie((total_sum, out))

    def close(meta):
        return near_pairs(meta, reach, one, two, x0, w0, cot, cot_theirs, lags)

    sums, (gate, inp, back, conv, adj) = stage(sums, "ch", (1, 2, 3), close)

    def finish(meta):
        return far_pairs(
            meta, reach, conv, adj, one, two, x2, w2, cot, cot_theirs, gate, inp, back, lags
        )

    sums, (gate, inp, back) = stage(sums, "ctx", (8, 16, 24), finish)
    got = swapped(back, "ctx", 1)
    sums, (gate, inp) = stage(sums, "ctx", (2, 4, 6), lambda meta: place_mine(meta, gate, inp))
    count = lax.axis_size("ctx")
    low = count // 8 - 1
    mirrored = [(a, a ^ (count - 1 - low)) for a in range(count)]
    moved = [
        lax.ppermute(sums, "ctx", mirrored),
        swapped(sums, "ctx", 1),
        lax.ppermute(sums, "ctx", [(a, b ^ 1) for a, b in mirrored]),
    ]
    return join(meta, got, gate, inp, sums, moved)


def solution(mesh):
    return jax.shard_map(
        per_device,
        mesh=mesh,
        in_specs=(P("ctx", None, "ch"), P("ctx", None, "ch"), P("ctx", None, "ch"), P(), P(), P()),
        out_specs=(P("ctx", None, "ch"), P("ctx", None, "ch"), P()),
        check_vma=False,
    )
```
